32 devices in a mesh: group: 4 (over z), dev: 8 (over y, x, core).
Axes of the slice: x: 2, y: 2, z: 4, core: 2. Of those that a mesh axis runs over, the one named last changes fastest.
Arguments:
- fine_state: float32 [5, 128, 16384], P(None, 'group', 'dev'), may hold values from -2 to 9.25, as said below
- coarse_boxes: float32 [4096, 5, 512], P(('group', 'dev')), may hold values from -2 to 9.25, as said below
- piece_owner: int32 [1024, 1], P(('group', 'dev')), may hold values from 0 to 7; in each aligned block of 32 rows (0 to 31, 32 to 63, ...) at most 8 rows name the same one
- piece_box: int32 [1024], P(('group', 'dev')), may hold values from 0 to 127
Outputs:
- fine_next: float32 [5, 128, 16384], P(None, 'group', 'dev')
- flux_register: float32 [5, 32, 4096], P(None, None, ('group', 'dev'))
The draws below stay inside these ranges and needn't reach their ends.
Inputs may be any that keep to these rules, and one draw needn't show every extreme that they name: `piece_owner`: among the pieces of one device no owner is named more than 8 times, and in some devices one owner is named exactly 8 times. `fine_state`: conserved variables of states with density in 0.5 to 2, velocity components in -1 to 1 and pressure in 0.4 to 2.5. `coarse_boxes`: conserved variables of states with density in 0.5 to 2, velocity components in -1 to 1 and pressure in 0.4 to 2.5.
All inputs are finite; a program needn't handle non-finite values.
Results may differ from the reference program's by a relative error of at most 0.0003.
Values sent between devices are 32-bit elements; how exact they have to be, the bound alone decides.
No kernel may reach another device: no remote copies, remote signals or barrier semaphores. Data moves between devices by JAX's collectives and lax.ppermute only.
A program may use at most 128 MiB of HBM per device.

```python
import math
import jax
import jax.numpy as jnp
import numpy as np
from jax import lax

PS = 16
RATIO = 4
QS = 16
PATCH_Y = 2
PATCH_X = 8
BOX_DEV = 128
CF = 4
CB = 8
PIECE_DEV = 32
MOST = 8
NXF = 1024
NYF = 128
PIECES = 1024
NBOX = 4096
N_GROUP = 4
N_DEV = 8
DEVICES = 32


def gas_sample(key, cells_shape):
    subkeys = jax.random.split(key, 5)
    density = jnp.exp(jax.random.uniform(subkeys[0], cells_shape, jnp.float32, math.log(0.5), math.log(2.0)))
    pressure = jnp.exp(jax.random.uniform(subkeys[4], cells_shape, jnp.float32, math.log(0.4), math.log(2.5)))
    density = jnp.clip(density, 0.5, 2.0)
    pressure = jnp.clip(pressure, 0.4, 2.5)
    velocity = [jax.random.uniform(subkeys[1 + number], cells_shape, jnp.float32, -1.0, 1.0) for number in range(3)]
    energy = pressure / 0.4 + 0.5 * density * (velocity[0] * velocity[0] + velocity[1] * velocity[1] + velocity[2] * velocity[2])
    return jnp.stack([density, density * velocity[0], density * velocity[1], density * velocity[2], energy])


def draw_fine_state(key, part):
    return gas_sample(jax.random.fold_in(key, 11), (NYF, NXF * PS)).astype(jnp.float32)


def draw_coarse_boxes(key, part):
    cells = gas_sample(jax.random.fold_in(key, 23), (NBOX, CB * CB * CB))
    return cells.transpose(1, 0, 2).astype(jnp.float32)


def plant(values, stream_key, least, high):
    longest = values.shape.index(max(values.shape))
    spots = []
    for shift in (0, 1):
        where = [jax.random.randint(jax.random.fold_in(stream_key, axis), (), 0, length) for axis, length in enumerate(values.shape)]
        where[longest] = (where[longest] + shift) % values.shape[longest]
        spots.append(tuple(where))
    return values.at[spots[0]].set(least).at[spots[1]].set(high)


def routed_block(rng, own, number, rows, amount, top, reach, lean):
    sequence = jax.random.permutation(rng, amount)
    crowded, usual = shares(amount, rows * top, reach, lean, True), shares(amount, rows * top, reach, lean, False)
    places = jnp.arange(amount)

    def named(tallies, turn):
        used = int((tallies > 0).sum())
        fixed = max(1, used // 4)
        moved = fixed + (places - fixed + turn * (used - fixed)) % max(1, amount - fixed)
        return jnp.zeros((amount,), jnp.int32).at[sequence[jnp.where(places < fixed, places, moved)]].set(jnp.asarray(tallies, jnp.int32))

    tallies = jnp.where(number % 4 == 0, named(crowded, number // 4), named(usual, number - number // 4 - 1))
    mixed = jax.random.permutation(jax.random.fold_in(own, 3), amount)
    source_of, sink = mixed[0:amount // 2 * 2:2], mixed[1:amount // 2 * 2:2]
    margin = jnp.minimum(tallies[source_of] - 1, reach - tallies[sink]) // 2
    margin = jnp.where((source_of == sequence[0]) | (sink == sequence[0]) | (tallies[sink] == 0), 0, jnp.maximum(margin, 0))
    moved = jax.random.randint(jax.random.fold_in(own, 4), (amount // 2,), 0, 1 << 20) % (margin + 1)
    tallies = tallies.at[source_of].add(-moved).at[sink].add(moved)
    members = jnp.searchsorted(jnp.cumsum(tallies), jnp.arange(rows * top), side="right").astype(jnp.int32)
    table = members.reshape(top, rows).T
    table = table[jax.random.permutation(jax.random.fold_in(own, 1), rows)]
    turn = jax.random.randint(jax.random.fold_in(own, 2), (rows, 1), 0, top)
    return jnp.take_along_axis(table, (jnp.arange(top)[None, :] + turn) % top, axis=1)


def shares(amount, total, reach, skew, full):
    weights = [(1 << 20) // math.isqrt(rank ** skew) + 1 for rank in range(1, amount + 1)]
    largest = reach if full else min(reach, max(-(-total // amount), total * weights[0] // sum(weights)))
    least = 1 if total - largest >= amount - 1 else 0
    given, spare = [largest] + [least] * (amount - 1), total - largest - least * (amount - 1)
    while spare > 0:
        free = [i for i in range(1, amount) if given[i] < largest] or [i for i in range(1, amount) if given[i] < reach]
        pool, remaining = sum([weights[i] for i in free]), spare
        for i in free:
            more = min(reach - given[i], max(1, remaining * weights[i] // pool), spare)
            given[i] = given[i] + more
            spare = spare - more
    return np.array(given)


def setup_inputs(seed: int = 0) -> dict:
    splits = jax.random.split(jax.random.key(seed), 5)
    fine_state = draw_fine_state(jax.random.fold_in(splits[4], 71), 0)
    coarse_boxes = draw_coarse_boxes(jax.random.fold_in(splits[4], 71), 0)
    piece_owner_keys = jax.random.split(jax.random.fold_in(splits[2], 1), PIECES // PIECE_DEV)
    piece_owner_turns = jax.random.permutation(jax.random.fold_in(splits[2], 3), PIECES // PIECE_DEV)
    piece_owner = jax.vmap(lambda own, number: routed_block(jax.random.fold_in(splits[2], 2), own, number, PIECE_DEV, N_DEV, 1, MOST, 2))(piece_owner_keys, piece_owner_turns).reshape((PIECES, 1))
    piece_box = plant(jax.random.randint(splits[3], (PIECES,), 0, BOX_DEV), jax.random.fold_in(splits[3], 1), 0, BOX_DEV - 1).astype(jnp.int32)
    return dict(fine_state=fine_state, coarse_boxes=coarse_boxes, piece_owner=piece_owner, piece_box=piece_box)


GAMMA = 1.4
DT_DX = 0.08

def minmod(lower_diff, upper_diff):
    return jnp.where(lower_diff * upper_diff > 0.0, jnp.where(jnp.abs(lower_diff) < jnp.abs(upper_diff), lower_diff, upper_diff), 0.0)

def to_primitive(conserved):
    density = conserved[0]
    momentum = conserved[1:4]
    kinetic = 0.5 * (momentum[0] * momentum[0] + momentum[1] * momentum[1] + momentum[2] * momentum[2]) / density
    pressure = (GAMMA - 1.0) * (conserved[4] - kinetic)
    return jnp.stack([density, momentum[0] / density, momentum[1] / density, momentum[2] / density, pressure])

def state_terms(primitive, normal):
    density = primitive[0]
    pressure = primitive[4]
    normal_speed = primitive[1 + normal]
    energy = pressure / (GAMMA - 1.0) + 0.5 * density * (primitive[1] * primitive[1] + primitive[2] * primitive[2] + primitive[3] * primitive[3])
    cons_list = [density, density * primitive[1], density * primitive[2], density * primitive[3], energy]
    flux_list = [element * normal_speed for element in cons_list]
    flux_list[1 + normal] = flux_list[1 + normal] + pressure
    flux_list[4] = flux_list[4] + pressure * normal_speed
    sound_speed = jnp.sqrt(GAMMA * pressure / density)
    return (jnp.stack(cons_list), jnp.stack(flux_list), normal_speed, sound_speed)

def hll_flux(lower_state, upper_state, normal):
    cons_low, flux_low, speed_low, sound_low = state_terms(lower_state, normal)
    cons_up, flux_up, speed_up, sound_up = state_terms(upper_state, normal)
    slowest = jnp.minimum(jnp.minimum(speed_low - sound_low, speed_up - sound_up), 0.0)
    fastest = jnp.maximum(jnp.maximum(speed_low + sound_low, speed_up + sound_up), 0.0)
    return (fastest * flux_low - slowest * flux_up + slowest * fastest * (cons_up - cons_low)) / (fastest - slowest)

def face_fluxes(primitive, lower_ghost, upper_ghost, dim_index, normal):
    length = primitive.shape[dim_index]

    def part_of(array, start, stop):
        return lax.slice_in_dim(array, start, stop, axis=dim_index)
    before = jnp.concatenate([part_of(lower_ghost, 1, 2), part_of(primitive, 0, length - 1)], axis=dim_index)
    before_two = jnp.concatenate([lower_ghost, part_of(primitive, 0, length - 2)], axis=dim_index)
    after = jnp.concatenate([part_of(primitive, 1, length), part_of(upper_ghost, 0, 1)], axis=dim_index)
    slopes = minmod(primitive - before, after - primitive)
    slopes_before = minmod(before - before_two, primitive - before)
    lower_faces = hll_flux(before + 0.5 * slopes_before, primitive - 0.5 * slopes, normal)
    last_cell = part_of(primitive, length - 1, length)
    ghost_near = part_of(upper_ghost, 0, 1)
    ghost_far = part_of(upper_ghost, 1, 2)
    ghost_slope = minmod(ghost_near - last_cell, ghost_far - ghost_near)
    end_face = hll_flux(last_cell + 0.5 * part_of(slopes, length - 1, length), ghost_near - 0.5 * ghost_slope, normal)
    upper_faces = jnp.concatenate([part_of(lower_faces, 1, length), end_face], axis=dim_index)
    return (upper_faces - lower_faces, lower_faces, end_face)

def advance(primitive, x_low, x_high, y_low, y_high, z_low, z_high):
    change = face_fluxes(primitive, x_low, x_high, 3, 0)[0] + face_fluxes(primitive, y_low, y_high, 1, 1)[0]
    z_change, z_lower, z_end = face_fluxes(primitive, z_low, z_high, 2, 2)
    return (change + z_change, z_lower[:, :, 0, :], z_end[:, :, 0, :])

def extract(box_cells, face_side):
    shaped = box_cells.reshape(box_cells.shape[:-1] + (CB, CB, CB))
    low_cut = shaped[..., CB - 4:CB - 1, 1:CB - 1, 1:CB - 1]
    high_cut = shaped[..., 1:4, 1:CB - 1, 1:CB - 1]
    return jnp.where((face_side == 1)[..., None, None, None, None], high_cut, low_cut)

def spread(values):
    return values[..., None, :, None, :, None]

def interpolate(coarse_cut, face_side):
    moved = jnp.moveaxis(coarse_cut, -4, 0)
    primitive = to_primitive(moved)
    centre = primitive[..., 1, 1:-1, 1:-1]
    slope_z = minmod(centre - primitive[..., 0, 1:-1, 1:-1], primitive[..., 2, 1:-1, 1:-1] - centre)
    slope_y = minmod(centre - primitive[..., 1, :-2, 1:-1], primitive[..., 1, 2:, 1:-1] - centre)
    slope_x = minmod(centre - primitive[..., 1, 1:-1, :-2], primitive[..., 1, 1:-1, 2:] - centre)
    offsets = (jnp.arange(RATIO, dtype=jnp.float32) + 0.5) / RATIO - 0.5
    z_offsets = jnp.where((face_side == 1)[..., None], offsets[:2], offsets[RATIO - 2:])
    fine = spread(centre) + spread(slope_z) * z_offsets[..., :, None, None, None, None]
    fine = fine + spread(slope_y) * offsets[:, None, None]
    fine = fine + spread(slope_x) * offsets
    fine = fine.reshape(fine.shape[:-5] + (2, QS, QS))
    return jnp.moveaxis(fine, 0, -4)

def assemble(pieces, face_index):
    chosen = pieces[:, :, face_index]
    return chosen.transpose(4, 0, 3, 6, 5, 1, 2, 7).reshape(5, PATCH_Y * PS, 2, PATCH_X * PS)

def coarsen(flux):
    across = PS // QS
    grouped = flux.reshape(5, PATCH_Y, across, CF, RATIO, PATCH_X, across, CF, RATIO)
    summed = grouped.sum(axis=(4, 8)) * (1.0 / RATIO)
    return summed.transpose(1, 4, 5, 2, 0, 3, 6)

def reference(fine_state, coarse_boxes, piece_owner, piece_box):
    across = PS // QS
    x_cells = PATCH_X * PS
    y_cells = PATCH_Y * PS
    conserved_all = fine_state.reshape(5, NYF, NXF, PS).transpose(0, 1, 3, 2)
    primitive_all = to_primitive(conserved_all)
    piece_ids = jnp.arange(PIECES, dtype=jnp.int32)
    device_ids = piece_ids // PIECE_DEV
    face_side = piece_ids % PIECE_DEV // (across * across) % 2
    box_index = (device_ids // N_DEV * N_DEV + piece_owner[:, 0]) * BOX_DEV + piece_box
    ghost_cells = interpolate(extract(coarse_boxes[box_index], face_side), face_side)
    ghost_by_device = ghost_cells.reshape(DEVICES, PATCH_Y, PATCH_X, 2, across, across, 5, 2, QS, QS)
    zero_index = jnp.zeros((), jnp.int32)

    def one_device(device):
        group_index = device // N_DEV
        dev_index = device % N_DEV
        y_start = (group_index * y_cells).astype(jnp.int32)
        x_start = (dev_index * x_cells).astype(jnp.int32)
        block = lax.dynamic_slice(primitive_all, (zero_index, y_start, zero_index, x_start), (5, y_cells, PS, x_cells))
        conserved_block = lax.dynamic_slice(conserved_all, (zero_index, y_start, zero_index, x_start), (5, y_cells, PS, x_cells))
        left_start = jnp.maximum(x_start - 2, 0).astype(jnp.int32)
        right_start = jnp.minimum(x_start + x_cells, NXF - 2).astype(jnp.int32)
        left_got = lax.dynamic_slice(primitive_all, (zero_index, y_start, zero_index, left_start), (5, y_cells, PS, 2))
        right_got = lax.dynamic_slice(primitive_all, (zero_index, y_start, zero_index, right_start), (5, y_cells, PS, 2))
        first_cell = block[..., :1]
        last_cell = block[..., x_cells - 1:]
        x_low = jnp.where(dev_index == 0, jnp.concatenate([first_cell, first_cell], axis=3), left_got)
        x_high = jnp.where(dev_index == N_DEV - 1, jnp.concatenate([last_cell, last_cell], axis=3), right_got)
        rows_low = ((y_start - 2 + jnp.arange(2, dtype=jnp.int32)) % NYF).astype(jnp.int32)
        rows_high = ((y_start + y_cells + jnp.arange(2, dtype=jnp.int32)) % NYF).astype(jnp.int32)
        y_low = lax.dynamic_slice_in_dim(jnp.take(primitive_all, rows_low, axis=1), x_start, x_cells, axis=3)
        y_high = lax.dynamic_slice_in_dim(jnp.take(primitive_all, rows_high, axis=1), x_start, x_cells, axis=3)
        pieces = ghost_by_device[device]
        z_low = assemble(pieces, 0)
        z_high = assemble(pieces, 1)
        change, bottom_flux, top_flux = advance(block, x_low, x_high, y_low, y_high, z_low, z_high)
        updated = conserved_block - DT_DX * change
        terms = jnp.stack([coarsen(bottom_flux), coarsen(top_flux)], axis=2).reshape(PIECE_DEV, 5 * CF * CF)
        return (updated, terms)
    updated, terms = lax.map(one_device, jnp.arange(DEVICES, dtype=jnp.int32))
    fine_next = updated.reshape(N_GROUP, N_DEV, 5, y_cells, PS, x_cells).transpose(2, 0, 3, 1, 5, 4).reshape(5, NYF, NXF * PS)
    segment_ids = face_side * NBOX + box_index
    summed = jax.ops.segment_sum(terms.reshape(PIECES, 5 * CF * CF), segment_ids, num_segments=2 * NBOX)
    flux_register = summed.reshape(2, NBOX, 5, CF * CF).transpose(2, 0, 3, 1).reshape(5, 2 * CF * CF, NBOX)
    return (fine_next, flux_register)
```

```python
import functools

import jax
import jax.numpy as jnp
from jax import lax
from jax.experimental import pallas as pl
from jax.experimental.pallas import tpu as pltpu
from jax.sharding import PartitionSpec as P

PS = 16
RATIO = 4
QS = 16
CF = 4
CB = 8
NF = 5
LANES = 128
ROWS = 8
SIDES = 2
QUANT = 4

GAMMA = 1.4
DT_DX = 0.08
OFFSETS = [(i + 0.5) / RATIO - 0.5 for i in range(RATIO)]
F32, BF16, I32 = jnp.float32, jnp.bfloat16, jnp.int32
TABLE_ROWS = NF * QUANT * CF * CF
TABLE_PAD = 384
TERM_ROWS = 32


def iota(shape, dim):
    return lax.broadcasted_iota(I32, shape, dim)


def minmod(a, b):
    return jnp.maximum(jnp.minimum(a, b), 0.0) + jnp.minimum(jnp.maximum(a, b), 0.0)


def to_primitive(cons):
    inverse = 1.0 / cons[0]
    velocity = [cons[1 + i] * inverse for i in range(3)]
    kinetic = cons[1] * velocity[0] + cons[2] * velocity[1] + cons[3] * velocity[2]
    return [cons[0]] + velocity + [(GAMMA - 1.0) * (cons[4] - 0.5 * kinetic)]


def hll(low, up, normal):
    others = [1 + i for i in range(3) if i != normal]
    u_low, u_up = low[1 + normal], up[1 + normal]
    p_low, p_up = low[4], up[4]
    g_low, g_up = GAMMA * p_low, GAMMA * p_up
    c_low = g_low * lax.rsqrt(g_low * low[0])
    c_up = g_up * lax.rsqrt(g_up * up[0])
    slow = jnp.minimum(jnp.minimum(u_low - c_low, u_up - c_up), 0.0)
    fast = jnp.maximum(jnp.maximum(u_low + c_low, u_up + c_up), 0.0)
    inverse = 1.0 / (fast - slow)
    f = fast * inverse
    s = slow * inverse
    a = f * (u_low - slow)
    b = s * (u_up - fast)
    m_low = a * low[0]
    m_up = b * up[0]
    k_low = 0.5 * (low[1] * low[1] + low[2] * low[2] + low[3] * low[3])
    k_up = 0.5 * (up[1] * up[1] + up[2] * up[2] + up[3] * up[3])
    rest = 1.0 / (GAMMA - 1.0)
    flux = [m_low - m_up, None, None, None, None]
    for i in others:
        flux[i] = m_low * low[i] - m_up * up[i]
    flux[1 + normal] = (m_low * u_low + f * p_low) - (m_up * u_up + s * p_up)
    flux[4] = (m_low * k_low + p_low * (rest * a + f * u_low)) - (
        m_up * k_up + p_up * (rest * b + s * u_up)
    )
    return flux


def split3(x):
    high = x.astype(BF16)
    left = x - high.astype(F32)
    middle = left.astype(BF16)
    low = (left - middle.astype(F32)).astype(BF16)
    return [high, middle, low]


def swap_groups(tiles, lane):
    tiles = list(tiles)
    bit = 0
    while (1 << bit) < len(tiles):
        step = 1 << bit
        upper = ((lane >> bit) & 1) == 1
        for i in range(len(tiles)):
            if not i & step:
                first, second = tiles[i], tiles[i + step]
                tiles[i] = jnp.where(upper, pltpu.roll(second, step, 1), first)
                tiles[i + step] = jnp.where(upper, second, pltpu.roll(first, LANES - step, 1))
        bit += 1
    return tiles


def count_slots(owner_ref, count_ref, members, capacity, pieces):
    for m in range(members):
        count_ref[m] = 0
    slots = []
    for p in range(pieces):
        owner = owner_ref[p, 0]
        rank = count_ref[owner]
        count_ref[owner] = rank + 1
        slots.append(owner * capacity + rank)
    return slots


def prep_kernel(members, capacity, boxes, owner_ref, box_ref, fine_ref, msg_ref, lo_ref, hi_ref, count_ref):
    me = lax.axis_index("dev")
    pieces = box_ref.shape[0]
    chunks = fine_ref.shape[2] // LANES
    blocks = fine_ref.shape[1] // ROWS
    lane = iota((ROWS, LANES), 1)
    sub = iota((ROWS, LANES), 0)
    slots = count_slots(owner_ref, count_ref, members, capacity, pieces)
    values = jnp.zeros((ROWS, LANES), I32)
    for p in range(pieces):
        values = jnp.where(lane == slots[p], box_ref[p] + (boxes * (p % SIDES) + 1), values)
    values = jnp.where(sub == 0, values, 0).astype(F32)
    mine = (lane >= me * capacity) & (lane < (me + 1) * capacity)
    for m in range(members):
        shift = lax.rem((me - m) * capacity + LANES * members, LANES)
        msg_ref[m, NF * ROWS :, :] = jnp.where(mine, pltpu.roll(values, shift, 1), 0.0)
    width = 2 * PS
    for f in range(NF):
        left = fine_ref[f, 0:ROWS, 0:LANES]
        right = pltpu.roll(fine_ref[f, 0:ROWS, (chunks - 1) * LANES :], width, 1)
        for g in range(1, blocks):
            rows = slice(g * ROWS, (g + 1) * ROWS)
            here = lane // width == g
            left = jnp.where(here, pltpu.roll(fine_ref[f, rows, 0:LANES], width * g, 1), left)
            edge = fine_ref[f, rows, (chunks - 1) * LANES :]
            shift = (width * (g + 1)) % LANES
            right = jnp.where(here, pltpu.roll(edge, shift, 1) if shift else edge, right)
        for m in range(members):
            below = jnp.full((ROWS, LANES), m, I32) < me
            msg_ref[m, f * ROWS : (f + 1) * ROWS, :] = jnp.where(below, left, right)
    for f in range(NF):
        for j in range(chunks // 4):
            low = high = None
            for k in range(4):
                c = slice((4 * j + k) * LANES, (4 * j + k + 1) * LANES)
                first = fine_ref[f, 0:ROWS, c]
                last = fine_ref[f, (blocks - 1) * ROWS :, c]
                first = pltpu.roll(first, 2 * k, 0) if k else first
                last = pltpu.roll(last, 2 * k + 2, 0) if k < 3 else last
                low = first if k == 0 else jnp.where(sub // 2 == k, first, low)
                high = last if k == 0 else jnp.where(sub // 2 == k, last, high)
            lo_ref[f, j * ROWS : (j + 1) * ROWS, :] = low
            hi_ref[f, j * ROWS : (j + 1) * ROWS, :] = high


def build_kernel(
    members, capacity, owner_ref, fine_ref, coarse_ref,
    wn_ref, wz_ref, zc_ref, tab_ref, he_ref,
    count_ref, ct_ref,
):
    lane = iota((ROWS, LANES), 1)
    sub = iota((ROWS, LANES), 0)
    chunks = fine_ref.shape[2] // LANES
    blocks = fine_ref.shape[1] // ROWS
    patch_y = fine_ref.shape[1] // PS
    patch_x = chunks * LANES // PS // PS
    pieces = owner_ref.shape[0]
    slot_count = members * capacity

    def primitive_block(block, carry):
        rows = pl.ds(pl.multiple_of(block * ROWS, ROWS), ROWS)
        for c in range(chunks):
            prim = to_primitive(
                [fine_ref[f, rows, c * LANES : (c + 1) * LANES] for f in range(NF)]
            )
            for f in range(NF):
                wn_ref[f, c, rows, :] = prim[f]
        return carry

    lax.fori_loop(0, blocks, primitive_block, 0)

    def turn(step, carry):
        f = step // blocks
        rows = pl.ds(pl.multiple_of((step % blocks) * ROWS, ROWS), ROWS)
        tiles = swap_groups([wn_ref[f, c, rows, :] for c in range(chunks)], lane)
        for z in range(PS):
            wz_ref[f, z, rows, :] = tiles[z]
        return carry

    lax.fori_loop(0, NF * blocks, turn, 0)

    def sweep(block, carry):
        rows = pl.ds(pl.multiple_of(block * ROWS, ROWS), ROWS)

        def load(z):
            return [wz_ref[f, z, rows, :] for f in range(NF)]

        w_here = load(1)
        w_before = load(0)
        diff = [w_here[f] - w_before[f] for f in range(NF)]
        low = flux = None
        for z in range(1, PS - 1):
            w_next = load(z + 1)
            diff_next = [w_next[f] - w_here[f] for f in range(NF)]
            half = [0.5 * minmod(diff[f], diff_next[f]) for f in range(NF)]
            if z >= 2:
                new = hll(low, [w_here[f] - half[f] for f in range(NF)], 2)
                for f in range(NF):
                    zc_ref[f, z - 2, rows, :] = new[f] if z == 2 else new[f] - flux[f]
                flux = new
            low = [w_here[f] + half[f] for f in range(NF)]
            w_here, diff = w_next, diff_next
        for f in range(NF):
            zc_ref[f, PS - 3, rows, :] = -flux[f]
        return carry

    lax.fori_loop(0, blocks, sweep, 0)

    slots = count_slots(owner_ref, count_ref, members, capacity, pieces)
    x_cell = (lane % PS) * (LANES // PS) + lane // PS
    for s in range(SIDES):
        for ky in range(patch_y):
            code = jnp.zeros((ROWS, LANES), I32)
            for kx in range(patch_x):
                slot = slots[(ky * patch_x + kx) * SIDES + s]
                code = jnp.where(x_cell // PS == kx, slot, code)
            code = code + (x_cell // RATIO) % CF * slot_count
            at = (s * patch_y + ky) * LANES
            hot = iota((CF * slot_count, LANES), 0) == code[0:1, :]
            he_ref[:, at : at + LANES] = jnp.where(hot, 1.0, 0.0).astype(BF16)

    boxes = coarse_ref.shape[0]
    for f in range(NF):
        for j in range(CB * CB * CB // LANES):
            at = slice(j * LANES, (j + 1) * LANES)
            ct_ref[f, at, :] = coarse_ref[:, f, at].T
    tab_ref[:, TABLE_ROWS:, :] = jnp.zeros((3, TABLE_PAD - TABLE_ROWS, SIDES * boxes), BF16)
    for s in range(SIDES):
        middle = CB - 3 if s == 0 else 2

        def cells(z, y):
            at = (z * CB + y) * CB
            return to_primitive([ct_ref[f, at : at + CB, :] for f in range(NF)])

        centre = {y: cells(middle, y) for y in range(1, CB - 1)}
        found = {}
        for cy in range(CF):
            y = cy + 2
            below, above = cells(middle - 1, y), cells(middle + 1, y)
            for f in range(NF):
                c = centre[y][f]
                found[f, 0, cy] = c
                found[f, 1, cy] = minmod(c - below[f], above[f] - c)
                found[f, 2, cy] = minmod(c - centre[y - 1][f], centre[y + 1][f] - c)
                found[f, 3, cy] = minmod(c - pltpu.roll(c, 1, 0), pltpu.roll(c, ROWS - 1, 0) - c)
        for f in range(NF):
            for q in range(QUANT):
                halves = [
                    jnp.where(
                        sub < CF,
                        pltpu.roll(found[f, q, 2 * i], ROWS - 2, 0),
                        pltpu.roll(found[f, q, 2 * i + 1], 2, 0),
                    )
                    for i in range(2)
                ]
                tile = jnp.concatenate(halves, axis=0)
                at = (f * QUANT + q) * CF * CF
                for number, part in enumerate(split3(tile)):
                    tab_ref[number, at : at + CF * CF, s * boxes : (s + 1) * boxes] = part


def serve_kernel(msg_ref, tab_ref, out_ref, hot_ref):
    members = msg_ref.shape[0]
    slot_count = out_ref.shape[0]
    row = msg_ref[0, NF * ROWS :, :]
    for m in range(1, members):
        row = row + msg_ref[m, NF * ROWS :, :]
    shape = (slot_count, LANES)
    wide = jnp.broadcast_to(row[0:1, :], shape)
    column = jnp.sum(jnp.where(iota(shape, 0) == iota(shape, 1), wide, 0.0), axis=1, keepdims=True)
    target = column.astype(I32) - 1
    hot = jnp.where(iota(hot_ref.shape, 1) == target, 1.0, 0.0).astype(BF16)
    hot_ref[...] = hot
    total = None
    for part in range(3):
        got = lax.dot_general(
            hot, tab_ref[part], (((1,), (1,)), ((), ())), preferred_element_type=F32
        )
        total = got if total is None else total + got
    out_ref[...] = total


def sweep_line(tiles, normal, back, forward, emit):
    fields = range(NF)
    last = len(tiles) - 1

    def join_back(before, here):
        return [back(before[f], here[f]) for f in fields]

    moved = [[back(None, t[f]) for f in fields] for t in tiles]
    diff = [
        [t[f] - back(moved[max(i - 1, 0)][f], moved[i][f]) for f in fields]
        for i, t in enumerate(tiles)
    ]
    diff_moved = [[forward(None, d[f]) for f in fields] for d in diff]
    low_moved = None
    flux = flux_moved = None
    for i, t in enumerate(tiles):
        half = [
            0.5 * minmod(diff[i][f], forward(diff_moved[i][f], diff_moved[min(i + 1, last)][f]))
            for f in fields
        ]
        low_next = [back(None, t[f] + half[f]) for f in fields]
        if i > 0:
            left = [back(low_moved[f], low_next[f]) for f in fields]
            new = hll(left, [t[f] - half[f] for f in fields], normal)
            new_moved = [forward(None, new[f]) for f in fields]
            if i > 1:
                emit(i - 2, [forward(flux_moved[f], new_moved[f]) - flux[f] for f in fields])
            flux, flux_moved = new, new_moved
        low_moved = low_next


def plane_kernel(members, msg_ref, lo_ref, hi_ref, wn_ref, out_ref):
    me = lax.axis_index("dev")
    chunks = wn_ref.shape[1]
    blocks = wn_ref.shape[2] // ROWS
    lane = iota((ROWS, LANES), 1)
    sub = iota((ROWS, LANES), 0)
    width = 2 * PS
    place = jnp.full((ROWS, LANES), me, I32)

    def x_back(before, here):
        if before is None:
            return pltpu.roll(here, PS, 1)
        return jnp.where(lane < PS, before, here)

    def x_forward(here, after):
        if here is None:
            return pltpu.roll(after, LANES - PS, 1)
        return jnp.where(lane >= LANES - PS, after, here)

    def x_block(block, carry):
        rows = pl.ds(pl.multiple_of(block * ROWS, ROWS), ROWS)
        left = jnp.maximum(me - 1, 0)
        right = jnp.minimum(me + 1, members - 1)
        shift_low = lax.rem(2 * LANES - width - width * block, LANES)
        shift_high = lax.rem(LANES - width * block, LANES)
        low = to_primitive(
            [pltpu.roll(msg_ref[left, f * ROWS : (f + 1) * ROWS, :], shift_low, 1) for f in range(NF)]
        )
        high = to_primitive(
            [pltpu.roll(msg_ref[right, f * ROWS : (f + 1) * ROWS, :], shift_high, 1) for f in range(NF)]
        )
        tiles = [[wn_ref[f, c, rows, :] for f in range(NF)] for c in range(chunks)]
        for f in range(NF):
            w = tiles[0][f]
            same = jnp.where(
                lane < LANES - PS, pltpu.roll(w, LANES - width, 1), pltpu.roll(w, LANES - PS, 1)
            )
            low[f] = jnp.where(place == 0, same, low[f])
            w = tiles[-1][f]
            same = jnp.where(lane < PS, pltpu.roll(w, PS, 1), pltpu.roll(w, width, 1))
            high[f] = jnp.where(place == members - 1, same, high[f])

        def emit(c, change):
            for f in range(NF):
                out_ref[f, c, rows, :] = change[f]

        sweep_line([low] + tiles + [high], 0, x_back, x_forward, emit)
        return carry

    lax.fori_loop(0, blocks, x_block, 0)

    def y_back(before, here):
        if before is None:
            return pltpu.roll(here, 1, 0)
        return jnp.where(sub < 1, before, here)

    def y_forward(here, after):
        if here is None:
            return pltpu.roll(after, ROWS - 1, 0)
        return jnp.where(sub >= ROWS - 1, after, here)

    def y_block(j, carry):
        rows = pl.ds(pl.multiple_of(j * ROWS, ROWS), ROWS)
        low = to_primitive([lo_ref[f, rows, :] for f in range(NF)])
        high = to_primitive([hi_ref[f, rows, :] for f in range(NF)])
        for k in range(4):
            c = 4 * j + k
            below = [pltpu.roll(t, (ROWS - 2 - 2 * k) % ROWS, 0) if k < 3 else t for t in low]
            above = [pltpu.roll(t, ROWS - 2 * k, 0) if k else t for t in high]
            tiles = [
                [wn_ref[f, c, b * ROWS : (b + 1) * ROWS, :] for f in range(NF)]
                for b in range(blocks)
            ]

            def emit(b, change):
                at = slice(b * ROWS, (b + 1) * ROWS)
                for f in range(NF):
                    out_ref[f, c, at, :] = out_ref[f, c, at, :] + change[f]

            sweep_line([below] + tiles + [above], 1, y_back, y_forward, emit)
        return carry

    lax.fori_loop(0, chunks // 4, y_block, 0)


def face_kernel(
    slot_count, got_ref, he_ref, wz_ref, zc_ref, term_ref, edge_ref,
    rt_ref, lf_ref, g_ref, fs_ref, v_ref,
):
    lane = iota((ROWS, LANES), 1)
    sub = iota((ROWS, LANES), 0)
    rows_all = NF * QUANT * CF
    y_cells = wz_ref.shape[2]
    blocks = y_cells // ROWS
    patch_y = y_cells // PS
    rt_ref[...] = got_ref[...].T
    for cx in range(CF):
        lf_ref[:, cx * slot_count : (cx + 1) * slot_count] = rt_ref[
            pl.ds(cx, rows_all, stride=CF), :
        ]
    parts = jnp.concatenate(split3(lf_ref[...]), axis=0)
    product = jnp.dot(parts, he_ref[...], preferred_element_type=F32)
    g_ref[...] = (
        product[0:rows_all] + product[rows_all : 2 * rows_all] + product[2 * rows_all :]
    )

    def pick(options, index):
        value = jnp.full((ROWS, LANES), options[0], F32)
        for i in range(1, RATIO):
            value = jnp.where(index == i, options[i], value)
        return value

    off_y = pick(OFFSETS, sub % RATIO)
    off_x = pick(OFFSETS, (lane // PS) % RATIO)
    for block in range(blocks):
        ky, half = block // (blocks // patch_y), block % (blocks // patch_y)
        rows = slice(block * ROWS, (block + 1) * ROWS)
        for s in range(SIDES):
            at = (s * patch_y + ky) * LANES
            ghosts = [[], []]
            for f in range(NF):
                terms = []
                for q in range(QUANT):
                    r = (f * QUANT + q) * CF + 2 * half
                    terms.append(
                        jnp.where(
                            sub < RATIO,
                            jnp.broadcast_to(g_ref[r : r + 1, at : at + LANES], (ROWS, LANES)),
                            jnp.broadcast_to(g_ref[r + 1 : r + 2, at : at + LANES], (ROWS, LANES)),
                        )
                    )
                for i in range(2):
                    off_z = OFFSETS[i + (RATIO - 2 if s == 0 else 0)]
                    ghosts[i].append(
                        ((terms[0] + terms[1] * off_z) + terms[2] * off_y) + terms[3] * off_x
                    )

            def load(z):
                return [wz_ref[f, z, rows, :] for f in range(NF)]

            if s == 0:
                line = ghosts + [load(0), load(1), load(2)]
            else:
                line = [load(PS - 3), load(PS - 2), load(PS - 1)] + ghosts
            diff = [[line[i + 1][f] - line[i][f] for f in range(NF)] for i in range(4)]
            half_slope = [
                [0.5 * minmod(diff[i][f], diff[i + 1][f]) for f in range(NF)] for i in range(3)
            ]
            flux = [
                hll(
                    [line[i + 1][f] + half_slope[i][f] for f in range(NF)],
                    [line[i + 2][f] - half_slope[i + 1][f] for f in range(NF)],
                    2,
                )
                for i in range(2)
            ]
            for f in range(NF):
                if s == 0:
                    edge_ref[f, 0, rows, :] = flux[1][f] - flux[0][f]
                    edge_ref[f, 1, rows, :] = zc_ref[f, 0, rows, :] - flux[1][f]
                    fs_ref[0, f, rows, :] = flux[0][f]
                else:
                    edge_ref[f, 2, rows, :] = zc_ref[f, PS - 3, rows, :] + flux[0][f]
                    edge_ref[f, 3, rows, :] = flux[1][f] - flux[0][f]
                    fs_ref[1, f, rows, :] = flux[1][f]

    v_ref[NF * CF :, :] = jnp.zeros((TERM_ROWS - NF * CF, v_ref.shape[1]), F32)
    for s in range(SIDES):
        for f in range(NF):
            total = None
            for i in range(RATIO):
                got = fs_ref[s, f, pl.ds(i, y_cells // RATIO, stride=RATIO), :]
                total = got if total is None else total + got
            total = total * (1.0 / RATIO)
            for ky in range(patch_y):
                at = (s * patch_y + ky) * LANES
                v_ref[f * CF : (f + 1) * CF, at : at + LANES] = total[ky * CF : (ky + 1) * CF]
    parts = jnp.concatenate(split3(v_ref[...]), axis=0)
    product = lax.dot_general(
        parts, he_ref[...], (((1,), (1,)), ((), ())), preferred_element_type=F32
    )
    summed = (
        product[0:TERM_ROWS] + product[TERM_ROWS : 2 * TERM_ROWS] + product[2 * TERM_ROWS :]
    )
    turned = summed.T
    for cx in range(CF):
        term_ref[:, cx * TERM_ROWS : (cx + 1) * TERM_ROWS] = turned[
            cx * slot_count : (cx + 1) * slot_count, :
        ]


def final_kernel(fine_ref, plane_ref, zc_ref, edge_ref, out_ref):
    lane = iota((ROWS, LANES), 1)
    chunks = plane_ref.shape[1]
    blocks = plane_ref.shape[2] // ROWS

    def turn(step, carry):
        f = step // blocks
        rows = pl.ds(pl.multiple_of((step % blocks) * ROWS, ROWS), ROWS)
        tiles = [edge_ref[f, 0, rows, :], edge_ref[f, 1, rows, :]]
        tiles += [zc_ref[f, z - 1, rows, :] for z in range(2, PS - 2)]
        tiles += [edge_ref[f, 2, rows, :], edge_ref[f, 3, rows, :]]
        tiles = swap_groups(tiles, lane)
        for c in range(chunks):
            at = slice(c * LANES, (c + 1) * LANES)
            change = plane_ref[f, c, rows, :] + tiles[c]
            out_ref[f, rows, at] = fine_ref[f, rows, at] - DT_DX * change
        return carry

    lax.fori_loop(0, NF * blocks, turn, 0)


def register_kernel(got_ref, hot_ref, out_ref, z_ref):
    boxes = out_ref.shape[2]
    turned = got_ref[...].T
    parts = jnp.concatenate(split3(turned), axis=0)
    product = jnp.dot(parts, hot_ref[...], preferred_element_type=F32)
    z_ref[...] = product[0:LANES] + product[LANES : 2 * LANES] + product[2 * LANES :]
    for f in range(NF):
        for cx in range(CF):
            at = cx * TERM_ROWS + f * CF
            for s in range(SIDES):
                out_ref[f, pl.ds(s * CF * CF + cx, CF, stride=CF), :] = z_ref[
                    at : at + CF, s * boxes : (s + 1) * boxes
                ]


VM = pl.BlockSpec(memory_space=pltpu.VMEM)
SM = pl.BlockSpec(memory_space=pltpu.SMEM)


def call(body, name, ins, outs, scratch=(), cost=0, limit=24):
    return pl.pallas_call(
        body,
        name=name,
        in_specs=list(ins),
        out_specs=[VM] * len(outs) if len(outs) > 1 else VM,
        out_shape=outs if len(outs) > 1 else outs[0],
        scratch_shapes=list(scratch),
        compiler_params=pltpu.CompilerParams(vmem_limit_bytes=limit << 20),
        cost_estimate=pl.CostEstimate(flops=cost, bytes_accessed=cost, transcendentals=0),
    )


def shaped(*shape, dtype=F32):
    return jax.ShapeDtypeStruct(shape, dtype)


def local(members, groups, fine_state, coarse_boxes, piece_owner, piece_box):
    y_cells = fine_state.shape[1]
    x_cells = fine_state.shape[2] // PS
    boxes = coarse_boxes.shape[0]
    pieces = piece_box.shape[0]
    capacity = max(4, 2 * pieces // members)
    slots = members * capacity
    chunks = x_cells * PS // LANES
    patch_y = y_cells // PS
    assert chunks == PS and boxes == LANES and slots <= LANES and PS == QS
    assert y_cells == 4 * ROWS and pieces == SIDES * patch_y * (x_cells // PS)
    edge_rows = 2 * chunks
    rows_all = NF * QUANT * CF
    wide = SIDES * patch_y * LANES
    count = pltpu.SMEM((members,), I32)

    msg, low_edge, high_edge = call(
        functools.partial(prep_kernel, members, capacity, boxes),
        "prep",
        (SM, SM, VM),
        [
            shaped(members, (NF + 1) * ROWS, LANES),
            shaped(NF, edge_rows, LANES),
            shaped(NF, edge_rows, LANES),
        ],
        [count],
        cost=1 << 18,
    )(piece_owner, piece_box, fine_state)
    got = lax.all_to_all(msg, "dev", split_axis=0, concat_axis=0, tiled=True)
    up = [(g, (g + 1) % groups) for g in range(groups)]
    down = [(b, a) for a, b in up]
    y_low = lax.ppermute(high_edge, "group", up)
    y_high = lax.ppermute(low_edge, "group", down)

    wn, wz, zc, table, hot_fine = call(
        functools.partial(build_kernel, members, capacity),
        "build",
        (SM, VM, VM),
        [
            shaped(NF, chunks, y_cells, LANES),
            shaped(NF, PS, y_cells, LANES),
            shaped(NF, PS - 2, y_cells, LANES),
            shaped(3, TABLE_PAD, SIDES * boxes, dtype=BF16),
            shaped(CF * slots, wide, dtype=BF16),
        ],
        [
            count,
            pltpu.VMEM((NF, CB * CB * CB, boxes), F32),
        ],
        cost=1 << 23,
    )(piece_owner, fine_state, coarse_boxes)

    payload, hot_box = call(
        serve_kernel,
        "serve",
        (VM, VM),
        [shaped(slots, TABLE_PAD), shaped(slots, SIDES * boxes, dtype=BF16)],
        cost=1 << 18,
    )(got, table)
    back = lax.all_to_all(payload, "dev", split_axis=0, concat_axis=0, tiled=True)

    plane = call(
        functools.partial(plane_kernel, members),
        "plane",
        (VM, VM, VM, VM),
        [shaped(NF, chunks, y_cells, LANES)],
        cost=1 << 24,
    )(got, y_low, y_high, wn)

    terms, edge = call(
        functools.partial(face_kernel, slots),
        "face",
        (VM, VM, VM, VM),
        [shaped(slots, LANES), shaped(NF, 4, y_cells, LANES)],
        [
            pltpu.VMEM((TABLE_PAD, slots), F32),
            pltpu.VMEM((rows_all, CF * slots), F32),
            pltpu.VMEM((rows_all, wide), F32),
            pltpu.VMEM((SIDES, NF, y_cells, LANES), F32),
            pltpu.VMEM((TERM_ROWS, wide), F32),
        ],
        cost=1 << 20,
    )(back, hot_fine, wz, zc)
    incoming = lax.all_to_all(terms, "dev", split_axis=0, concat_axis=0, tiled=True)

    fine_next = call(
        final_kernel,
        "final",
        (VM, VM, VM, VM),
        [shaped(*fine_state.shape)],
        cost=1 << 23,
    )(fine_state, plane, zc, edge)
    flux_register = call(
        register_kernel,
        "register",
        (VM, VM),
        [shaped(NF, SIDES * CF * CF, boxes)],
        [pltpu.VMEM((LANES, SIDES * boxes), F32)],
        cost=1 << 18,
    )(incoming, hot_box)
    return (fine_next, flux_register)


def solution(mesh):
    in_specs = (
        P(None, "group", "dev"),
        P(("group", "dev"), None, None),
        P(("group", "dev"), None),
        P(("group", "dev")),
    )
    out_specs = (P(None, "group", "dev"), P(None, None, ("group", "dev")))
    body = functools.partial(local, mesh.shape["dev"], mesh.shape["group"])
    return jax.shard_map(body, mesh=mesh, in_specs=in_specs, out_specs=out_specs, check_vma=False)
```

```python
import functools

import jax
import jax.numpy as jnp
from jax import lax
from jax.experimental import pallas as pl
from jax.experimental.pallas import tpu as pltpu
from jax.sharding import PartitionSpec as P

PS = 16
RATIO = 4
QS = 16
CF = 4
CB = 8
NF = 5
LANES = 128
ROWS = 8
SIDES = 2
QUANT = 4

GAMMA = 1.4
DT_DX = 0.08
OFFSETS = [(i + 0.5) / RATIO - 0.5 for i in range(RATIO)]
F32, BF16, I32 = jnp.float32, jnp.bfloat16, jnp.int32
TABLE_ROWS = NF * QUANT * CF * CF
TABLE_PAD = 384
TERM_ROWS = 32


def iota(shape, dim):
    return lax.broadcasted_iota(I32, shape, dim)


def minmod(a, b):
    return jnp.maximum(jnp.minimum(a, b), 0.0) + jnp.minimum(jnp.maximum(a, b), 0.0)


def to_primitive(cons):
    inverse = 1.0 / cons[0]
    velocity = [cons[1 + i] * inverse for i in range(3)]
    kinetic = cons[1] * velocity[0] + cons[2] * velocity[1] + cons[3] * velocity[2]
    return [cons[0]] + velocity + [(GAMMA - 1.0) * (cons[4] - 0.5 * kinetic)]


def hll(low, up, normal):
    others = [1 + i for i in range(3) if i != normal]
    u_low, u_up = low[1 + normal], up[1 + normal]
    p_low, p_up = low[4], up[4]
    g_low, g_up = GAMMA * p_low, GAMMA * p_up
    c_low = g_low * lax.rsqrt(g_low * low[0])
    c_up = g_up * lax.rsqrt(g_up * up[0])
    slow = jnp.minimum(jnp.minimum(u_low - c_low, u_up - c_up), 0.0)
    fast = jnp.maximum(jnp.maximum(u_low + c_low, u_up + c_up), 0.0)
    inverse = 1.0 / (fast - slow)
    f = fast * inverse
    s = slow * inverse
    a = f * (u_low - slow)
    b = s * (u_up - fast)
    m_low = a * low[0]
    m_up = b * up[0]
    k_low = 0.5 * (low[1] * low[1] + low[2] * low[2] + low[3] * low[3])
    k_up = 0.5 * (up[1] * up[1] + up[2] * up[2] + up[3] * up[3])
    rest = 1.0 / (GAMMA - 1.0)
    flux = [m_low - m_up, None, None, None, None]
    for i in others:
        flux[i] = m_low * low[i] - m_up * up[i]
    flux[1 + normal] = (m_low * u_low + f * p_low) - (m_up * u_up + s * p_up)
    flux[4] = (m_low * k_low + p_low * (rest * a + f * u_low)) - (
        m_up * k_up + p_up * (rest * b + s * u_up)
    )
    return flux


def split3(x):
    high = x.astype(BF16)
    left = x - high.astype(F32)
    middle = left.astype(BF16)
    low = (left - middle.astype(F32)).astype(BF16)
    return [high, middle, low]


def swap_groups(tiles, lane):
    tiles = list(tiles)
    bit = 0
    while (1 << bit) < len(tiles):
        step = 1 << bit
        upper = ((lane >> bit) & 1) == 1
        for i in range(len(tiles)):
            if not i & step:
                first, second = tiles[i], tiles[i + step]
                tiles[i] = jnp.where(upper, pltpu.roll(second, step, 1), first)
                tiles[i + step] = jnp.where(upper, second, pltpu.roll(first, LANES - step, 1))
        bit += 1
    return tiles


def count_slots(owner_ref, count_ref, members, capacity, pieces):
    for m in range(members):
        count_ref[m] = 0
    slots = []
    for p in range(pieces):
        owner = owner_ref[p]
        rank = count_ref[owner]
        count_ref[owner] = rank + 1
        slots.append(owner * capacity + rank)
    return slots


def prep_kernel(
    members, capacity, boxes, owner_hbm, box_hbm, fine_hbm, msg_hbm, lo_hbm, hi_hbm, code_ref,
    owner_ref, box_ref, count_ref, low_ref, high_ref, left_ref, right_ref,
    msg_ref, lo_ref, hi_ref, sem_ref, out_sem,
):
    me = lax.axis_index("dev")
    pieces = box_hbm.shape[0]
    y_cells = fine_hbm.shape[1]
    chunks = fine_hbm.shape[2] // LANES
    blocks = y_cells // ROWS
    ends = [
        (owner_hbm, owner_ref),
        (box_hbm, box_ref),
        (fine_hbm.at[:, :, 0:LANES], left_ref),
        (fine_hbm.at[:, :, (chunks - 1) * LANES : chunks * LANES], right_ref),
        (fine_hbm.at[:, 0:ROWS, :], low_ref),
        (fine_hbm.at[:, y_cells - ROWS : y_cells, :], high_ref),
    ]
    copies = [pltpu.make_async_copy(a, b, sem_ref.at[i]) for i, (a, b) in enumerate(ends)]
    for copy in copies:
        copy.start()
    lane = iota((ROWS, LANES), 1)
    sub = iota((ROWS, LANES), 0)
    copies[0].wait()
    copies[1].wait()
    slots = count_slots(owner_ref, count_ref, members, capacity, pieces)
    values = jnp.zeros((ROWS, LANES), I32)
    for p in range(pieces):
        values = jnp.where(lane == slots[p], box_ref[p] + (boxes * (p % SIDES) + 1), values)
    values = jnp.where(sub == 0, values, 0).astype(F32)
    mine = (lane >= me * capacity) & (lane < (me + 1) * capacity)
    for m in range(members):
        shift = lax.rem((me - m) * capacity + LANES * members, LANES)
        msg_ref[m, NF * ROWS :, :] = jnp.where(mine, pltpu.roll(values, shift, 1), 0.0)
    width = 2 * PS
    copies[2].wait()
    copies[3].wait()
    for f in range(NF):
        left = left_ref[f, 0:ROWS, :]
        right = pltpu.roll(right_ref[f, 0:ROWS, :], width, 1)
        for g in range(1, blocks):
            rows = slice(g * ROWS, (g + 1) * ROWS)
            here = lane // width == g
            left = jnp.where(here, pltpu.roll(left_ref[f, rows, :], width * g, 1), left)
            edge = right_ref[f, rows, :]
            shift = (width * (g + 1)) % LANES
            right = jnp.where(here, pltpu.roll(edge, shift, 1) if shift else edge, right)
        for m in range(members):
            below = jnp.full((ROWS, LANES), m, I32) < me
            msg_ref[m, f * ROWS : (f + 1) * ROWS, :] = jnp.where(below, left, right)
    outs = [pltpu.make_async_copy(msg_ref, msg_hbm, out_sem.at[0])]
    outs[0].start()
    patch_y = y_cells // PS
    patch_x = chunks * LANES // PS // PS
    x_cell = (lane % PS) * (LANES // PS) + lane // PS
    for s in range(SIDES):
        for ky in range(patch_y):
            code = jnp.zeros((ROWS, LANES), I32)
            for kx in range(patch_x):
                slot = slots[(ky * patch_x + kx) * SIDES + s]
                code = jnp.where(x_cell // PS == kx, slot, code)
            code_ref[s * patch_y + ky] = code + (x_cell // RATIO) % CF * (members * capacity)
    copies[4].wait()
    copies[5].wait()
    for f in range(NF):
        for j in range(chunks // 4):
            low = high = None
            for k in range(4):
                c = slice((4 * j + k) * LANES, (4 * j + k + 1) * LANES)
                first = low_ref[f, :, c]
                last = high_ref[f, :, c]
                first = pltpu.roll(first, 2 * k, 0) if k else first
                last = pltpu.roll(last, 2 * k + 2, 0) if k < 3 else last
                low = first if k == 0 else jnp.where(sub // 2 == k, first, low)
                high = last if k == 0 else jnp.where(sub // 2 == k, last, high)
            lo_ref[f, j * ROWS : (j + 1) * ROWS, :] = low
            hi_ref[f, j * ROWS : (j + 1) * ROWS, :] = high
    outs.append(pltpu.make_async_copy(lo_ref, lo_hbm, out_sem.at[1]))
    outs.append(pltpu.make_async_copy(hi_ref, hi_hbm, out_sem.at[2]))
    outs[1].start()
    outs[2].start()
    for copy in outs:
        copy.wait()


def build_kernel(fine_ref, coarse_hbm, wz_ref, tab_ref, wn_ref, cs_ref, ct_ref, coarse_sem):
    chunks = fine_ref.shape[2] // LANES
    blocks = fine_ref.shape[1] // ROWS
    coarse_copies = [
        pltpu.make_async_copy(coarse_hbm.at[f], cs_ref.at[f], coarse_sem.at[f]) for f in range(NF)
    ]
    for copy in coarse_copies:
        copy.start()
    lane = iota((ROWS, LANES), 1)
    sub = iota((ROWS, LANES), 0)

    def turn(block, carry):
        rows = pl.ds(pl.multiple_of(block * ROWS, ROWS), ROWS)
        for c in range(chunks):
            prim = to_primitive(
                [fine_ref[f, rows, c * LANES : (c + 1) * LANES] for f in range(NF)]
            )
            for f in range(NF):
                wn_ref[f, c] = prim[f]
        for f in range(NF):
            tiles = swap_groups([wn_ref[f, c] for c in range(chunks)], lane)
            for z in range(PS):
                wz_ref[f, z, rows, :] = tiles[z]
        return carry

    lax.fori_loop(0, blocks, turn, 0)

    boxes = coarse_hbm.shape[1]
    for f in range(NF):
        coarse_copies[f].wait()
        for j in range(CB * CB * CB // LANES):
            at = slice(j * LANES, (j + 1) * LANES)
            ct_ref[f, at, :] = cs_ref[f, :, at].T
    tab_ref[TABLE_ROWS:, :] = jnp.zeros((TABLE_PAD - TABLE_ROWS, SIDES * boxes), F32)
    for s in range(SIDES):
        middle = CB - 3 if s == 0 else 2

        def cells(z, y):
            at = (z * CB + y) * CB
            return to_primitive([ct_ref[f, at : at + CB, :] for f in range(NF)])

        centre = {y: cells(middle, y) for y in range(1, CB - 1)}
        found = {}
        for cy in range(CF):
            y = cy + 2
            below, above = cells(middle - 1, y), cells(middle + 1, y)
            for f in range(NF):
                c = centre[y][f]
                found[f, 0, cy] = c
                found[f, 1, cy] = minmod(c - below[f], above[f] - c)
                found[f, 2, cy] = minmod(c - centre[y - 1][f], centre[y + 1][f] - c)
                found[f, 3, cy] = minmod(c - pltpu.roll(c, 1, 0), pltpu.roll(c, ROWS - 1, 0) - c)
        for f in range(NF):
            for q in range(QUANT):
                at = (f * QUANT + q) * CF * CF
                for i in range(2):
                    tab_ref[at + i * ROWS : at + (i + 1) * ROWS, s * boxes : (s + 1) * boxes] = (
                        jnp.where(
                            sub < CF,
                            pltpu.roll(found[f, q, 2 * i], ROWS - 2, 0),
                            pltpu.roll(found[f, q, 2 * i + 1], 2, 0),
                        )
                    )


def serve_kernel(msg_ref, tab_ref, out_hbm, hot_ref, out_ref, sem_ref):
    members = msg_ref.shape[0]
    slot_count = out_ref.shape[0]
    row = msg_ref[0, NF * ROWS :, :]
    for m in range(1, members):
        row = row + msg_ref[m, NF * ROWS :, :]
    shape = (slot_count, LANES)
    wide = jnp.broadcast_to(row[0:1, :], shape)
    column = jnp.sum(jnp.where(iota(shape, 0) == iota(shape, 1), wide, 0.0), axis=1, keepdims=True)
    target = column.astype(I32) - 1
    hot = jnp.where(iota(hot_ref.shape, 1) == target, 1.0, 0.0).astype(BF16)
    hot_ref[...] = hot
    total = None
    for part in split3(tab_ref[...]):
        got = lax.dot_general(
            hot, part, (((1,), (1,)), ((), ())), preferred_element_type=F32
        )
        total = got if total is None else total + got
    out_ref[...] = total
    copy = pltpu.make_async_copy(out_ref, out_hbm, sem_ref.at[0])
    copy.start()
    copy.wait()


def sweep_line(tiles, normal, back, forward, emit, finish=None):
    fields = range(NF)
    last = len(tiles) - 1
    moved = [[back(None, t[f]) for f in fields] for t in tiles]
    diff = [
        [t[f] - back(moved[max(i - 1, 0)][f], moved[i][f]) for f in fields]
        for i, t in enumerate(tiles)
    ]
    diff_moved = [[forward(None, d[f]) for f in fields] for d in diff]
    low_moved = None
    flux = flux_moved = None
    for i, t in enumerate(tiles):
        half = [
            0.5 * minmod(diff[i][f], forward(diff_moved[i][f], diff_moved[min(i + 1, last)][f]))
            for f in fields
        ]
        if i == last and finish is not None:
            finish(low_moved, [t[f] - half[f] for f in fields], flux, flux_moved)
            return
        low_next = [back(None, t[f] + half[f]) for f in fields]
        if i > 0:
            left = [back(low_moved[f], low_next[f]) for f in fields]
            new = hll(left, [t[f] - half[f] for f in fields], normal)
            new_moved = [forward(None, new[f]) for f in fields]
            if i > 1:
                emit(i - 2, [forward(flux_moved[f], new_moved[f]) - flux[f] for f in fields])
            flux, flux_moved = new, new_moved
        low_moved = low_next


def plane_kernel(
    members, msg_ref, lo_ref, hi_ref, fine_ref, after_ref, out_ref, wn_ref
):
    me = lax.axis_index("dev")
    chunks = fine_ref.shape[2] // LANES
    blocks = fine_ref.shape[1] // ROWS
    lane = iota((ROWS, LANES), 1)
    sub = iota((ROWS, LANES), 0)
    width = 2 * PS
    place = jnp.full((ROWS, LANES), me, I32)

    def x_back(before, here):
        if before is None:
            return pltpu.roll(here, PS, 1)
        return jnp.where(lane < PS, before, here)

    def x_forward(here, after):
        if here is None:
            return pltpu.roll(after, LANES - PS, 1)
        return jnp.where(lane >= LANES - PS, after, here)

    def x_block(block, carry):
        rows = pl.ds(pl.multiple_of(block * ROWS, ROWS), ROWS)
        left = jnp.maximum(me - 1, 0)
        right = jnp.minimum(me + 1, members - 1)
        shift_low = lax.rem(2 * LANES - width - width * block, LANES)
        shift_high = lax.rem(LANES - width * block, LANES)
        low = to_primitive(
            [pltpu.roll(msg_ref[left, f * ROWS : (f + 1) * ROWS, :], shift_low, 1) for f in range(NF)]
        )
        high = to_primitive(
            [pltpu.roll(msg_ref[right, f * ROWS : (f + 1) * ROWS, :], shift_high, 1) for f in range(NF)]
        )
        tiles = []
        for c in range(chunks):
            prim = to_primitive(
                [fine_ref[f, rows, c * LANES : (c + 1) * LANES] for f in range(NF)]
            )
            for f in range(NF):
                wn_ref[f, c, rows, :] = prim[f]
            tiles.append(prim)
        for f in range(NF):
            w = tiles[0][f]
            same = jnp.where(
                lane < LANES - PS, pltpu.roll(w, LANES - width, 1), pltpu.roll(w, LANES - PS, 1)
            )
            low[f] = jnp.where(place == 0, same, low[f])
            w = tiles[-1][f]
            same = jnp.where(lane < PS, pltpu.roll(w, PS, 1), pltpu.roll(w, width, 1))
            high[f] = jnp.where(place == members - 1, same, high[f])

        def emit(c, change):
            at = slice(c * LANES, (c + 1) * LANES)
            for f in range(NF):
                out_ref[f, c, rows, :] = fine_ref[f, rows, at] - DT_DX * change[f]

        sweep_line([low] + tiles + [high], 0, x_back, x_forward, emit)
        return carry

    lax.fori_loop(0, blocks, x_block, 0)

    def y_back(before, here):
        if before is None:
            return pltpu.roll(here, 1, 0)
        return jnp.where(sub < 1, before, here)

    def y_forward(here, after):
        if here is None:
            return pltpu.roll(after, ROWS - 1, 0)
        return jnp.where(sub >= ROWS - 1, after, here)

    def y_block(j, carry):
        ends = []
        for k in range(ROWS):
            at = pl.ds(pl.multiple_of((2 * j + k // 4) * ROWS, ROWS), ROWS)
            if k % 4 == 0:
                low = to_primitive([lo_ref[f, at, :] for f in range(NF)])
                high = to_primitive([hi_ref[f, at, :] for f in range(NF)])
            c = ROWS * j + k
            turn_low, turn_high = (6 - 2 * (k % 4)) % ROWS, (ROWS - 2 * (k % 4)) % ROWS
            below = [pltpu.roll(t, turn_low, 0) if turn_low else t for t in low]
            above = [pltpu.roll(t, turn_high, 0) if turn_high else t for t in high]
            tiles = [
                [wn_ref[f, c, b * ROWS : (b + 1) * ROWS, :] for f in range(NF)]
                for b in range(blocks)
            ]

            def emit(b, change):
                at = slice(b * ROWS, (b + 1) * ROWS)
                for f in range(NF):
                    out_ref[f, c, at, :] = out_ref[f, c, at, :] - DT_DX * change[f]

            sweep_line(
                [below] + tiles + [above], 1, y_back, y_forward, emit, lambda *end: ends.append(end)
            )
        packed = []
        for which in range(2):
            state = []
            for f in range(NF):
                tile = ends[0][which][f]
                for k in range(1, ROWS):
                    tile = jnp.where(sub == k, pltpu.roll(ends[k][which][f], k, 0), tile)
                state.append(tile)
            packed.append(state)
        top = hll(packed[0], packed[1], 1)
        at = slice((blocks - 1) * ROWS, blocks * ROWS)
        for k in range(ROWS):
            c = ROWS * j + k
            flux, flux_moved = ends[k][2], ends[k][3]
            for f in range(NF):
                moved = pltpu.roll(top[f], ROWS - 1 - k, 0) if k < ROWS - 1 else top[f]
                change = y_forward(flux_moved[f], moved) - flux[f]
                out_ref[f, c, at, :] = out_ref[f, c, at, :] - DT_DX * change
        return carry

    lax.fori_loop(0, chunks // ROWS, y_block, 0)


def face_kernel(
    slot_count, got_ref, code_ref, wz_ref, after_ref, term_hbm, edge_ref,
    he_ref, rt_ref, lf_ref, g_ref, fs_ref, v_ref, term_ref, sem_ref,
):
    lane = iota((ROWS, LANES), 1)
    sub = iota((ROWS, LANES), 0)
    rows_all = NF * QUANT * CF
    y_cells = wz_ref.shape[2]
    blocks = y_cells // ROWS
    patch_y = y_cells // PS
    number = iota((CF * slot_count, LANES), 0)
    for i in range(code_ref.shape[0]):
        hot = jnp.where(number == code_ref[i, 0:1, :], 1.0, 0.0)
        he_ref[:, i * LANES : (i + 1) * LANES] = hot.astype(BF16)
    rt_ref[...] = got_ref[...].T
    for cx in range(CF):
        lf_ref[:, cx * slot_count : (cx + 1) * slot_count] = rt_ref[
            pl.ds(cx, rows_all, stride=CF), :
        ]
    parts = jnp.concatenate(split3(lf_ref[...]), axis=0)
    product = jnp.dot(parts, he_ref[...], preferred_element_type=F32)
    g_ref[...] = (
        product[0:rows_all] + product[rows_all : 2 * rows_all] + product[2 * rows_all :]
    )

    def pick(options, index):
        value = jnp.full((ROWS, LANES), options[0], F32)
        for i in range(1, RATIO):
            value = jnp.where(index == i, options[i], value)
        return value

    off_y = pick(OFFSETS, sub % RATIO)
    off_x = pick(OFFSETS, (lane // PS) % RATIO)
    for block in range(blocks):
        ky, half = block // (blocks // patch_y), block % (blocks // patch_y)
        rows = slice(block * ROWS, (block + 1) * ROWS)
        for s in range(SIDES):
            at = (s * patch_y + ky) * LANES
            ghosts = [[], []]
            for f in range(NF):
                terms = []
                for q in range(QUANT):
                    r = (f * QUANT + q) * CF + 2 * half
                    terms.append(
                        jnp.where(
                            sub < RATIO,
                            jnp.broadcast_to(g_ref[r : r + 1, at : at + LANES], (ROWS, LANES)),
                            jnp.broadcast_to(g_ref[r + 1 : r + 2, at : at + LANES], (ROWS, LANES)),
                        )
                    )
                for i in range(2):
                    off_z = OFFSETS[i + (RATIO - 2 if s == 0 else 0)]
                    ghosts[i].append(
                        ((terms[0] + terms[1] * off_z) + terms[2] * off_y) + terms[3] * off_x
                    )

            inner = [
                [wz_ref[f, z, rows, :] for f in range(NF)]
                for z in (range(3) if s == 0 else range(PS - 3, PS))
            ]
            line = ghosts + inner if s == 0 else inner + ghosts
            diff = [[line[i + 1][f] - line[i][f] for f in range(NF)] for i in range(4)]
            half_slope = [
                [0.5 * minmod(diff[i][f], diff[i + 1][f]) for f in range(NF)] for i in range(3)
            ]
            flux = [
                hll(
                    [line[i + 1][f] + half_slope[i][f] for f in range(NF)],
                    [line[i + 2][f] - half_slope[i + 1][f] for f in range(NF)],
                    2,
                )
                for i in range(2)
            ]
            for f in range(NF):
                if s == 0:
                    edge_ref[f, 0, rows, :] = flux[1][f] - flux[0][f]
                    edge_ref[f, 1, rows, :] = -flux[1][f]
                    fs_ref[0, f, rows, :] = flux[0][f]
                else:
                    edge_ref[f, 2, rows, :] = flux[0][f]
                    edge_ref[f, 3, rows, :] = flux[1][f] - flux[0][f]
                    fs_ref[1, f, rows, :] = flux[1][f]

    v_ref[NF * CF :, :] = jnp.zeros((TERM_ROWS - NF * CF, v_ref.shape[1]), F32)
    for s in range(SIDES):
        for f in range(NF):
            total = None
            for i in range(RATIO):
                got = fs_ref[s, f, pl.ds(i, y_cells // RATIO, stride=RATIO), :]
                total = got if total is None else total + got
            total = total * (1.0 / RATIO)
            for ky in range(patch_y):
                at = (s * patch_y + ky) * LANES
                v_ref[f * CF : (f + 1) * CF, at : at + LANES] = total[ky * CF : (ky + 1) * CF]
    parts = jnp.concatenate(split3(v_ref[...]), axis=0)
    product = lax.dot_general(
        parts, he_ref[...], (((1,), (1,)), ((), ())), preferred_element_type=F32
    )
    summed = (
        product[0:TERM_ROWS] + product[TERM_ROWS : 2 * TERM_ROWS] + product[2 * TERM_ROWS :]
    )
    turned = summed.T
    for cx in range(CF):
        term_ref[:, cx * TERM_ROWS : (cx + 1) * TERM_ROWS] = turned[
            cx * slot_count : (cx + 1) * slot_count, :
        ]
    copy = pltpu.make_async_copy(term_ref, term_hbm, sem_ref.at[0])
    copy.start()
    copy.wait()


def final_kernel(
    wz_ref, plane_ref, edge_ref, out_hbm, zc_ref, out_ref, out_sem
):
    lane = iota((ROWS, LANES), 1)
    chunks = plane_ref.shape[1]
    blocks = plane_ref.shape[2] // ROWS

    def out_copy(block):
        rows = pl.ds(pl.multiple_of(block * ROWS, ROWS), ROWS)
        return pltpu.make_async_copy(
            out_ref.at[:, rows, :], out_hbm.at[:, rows, :], out_sem.at[block]
        )

    def step(block, carry):
        rows = pl.ds(pl.multiple_of(block * ROWS, ROWS), ROWS)

        def load(z):
            return [wz_ref[f, z, rows, :] for f in range(NF)]

        w_here = load(1)
        w_before = load(0)
        diff = [w_here[f] - w_before[f] for f in range(NF)]
        low = flux = None
        for z in range(1, PS - 1):
            w_next = load(z + 1)
            diff_next = [w_next[f] - w_here[f] for f in range(NF)]
            half = [0.5 * minmod(diff[f], diff_next[f]) for f in range(NF)]
            if z >= 2:
                new = hll(low, [w_here[f] - half[f] for f in range(NF)], 2)
                for f in range(NF):
                    before = edge_ref[f, 1, rows, :] if z == 2 else -flux[f]
                    zc_ref[f, z - 2] = new[f] + before
                flux = new
            low = [w_here[f] + half[f] for f in range(NF)]
            w_here, diff = w_next, diff_next
        for f in range(NF):
            zc_ref[f, PS - 3] = edge_ref[f, 2, rows, :] - flux[f]
        for f in range(NF):
            tiles = [edge_ref[f, 0, rows, :]]
            tiles += [zc_ref[f, z] for z in range(PS - 2)]
            tiles += [edge_ref[f, 3, rows, :]]
            tiles = swap_groups(tiles, lane)
            for c in range(chunks):
                at = slice(c * LANES, (c + 1) * LANES)
                out_ref[f, rows, at] = plane_ref[f, c, rows, :] - DT_DX * tiles[c]
        out_copy(block).start()
        return carry

    lax.fori_loop(0, blocks, step, 0)
    for block in range(blocks):
        out_copy(block).wait()


def register_kernel(got_ref, hot_ref, out_ref, z_ref):
    boxes = out_ref.shape[2]
    turned = got_ref[...].T
    parts = jnp.concatenate(split3(turned), axis=0)
    product = jnp.dot(parts, hot_ref[...], preferred_element_type=F32)
    z_ref[...] = product[0:LANES] + product[LANES : 2 * LANES] + product[2 * LANES :]
    for f in range(NF):
        for cx in range(CF):
            at = cx * TERM_ROWS + f * CF
            for s in range(SIDES):
                out_ref[f, pl.ds(s * CF * CF + cx, CF, stride=CF), :] = z_ref[
                    at : at + CF, s * boxes : (s + 1) * boxes
                ]


VM = pl.BlockSpec(memory_space=pltpu.VMEM)
HB = pl.BlockSpec(memory_space=pltpu.HBM)


LIMITS = (65472, 60 * 1024, 16384, 16384, 16384, 16384, 16384)


def call(body, name, ins, outs, out_specs, scratch=(), cost=0, limit=16):
    return pl.pallas_call(
        body,
        name=name,
        in_specs=list(ins),
        out_specs=list(out_specs),
        out_shape=list(outs),
        scratch_shapes=list(scratch),
        compiler_params=pltpu.CompilerParams(vmem_limit_bytes=limit << 10),
        cost_estimate=pl.CostEstimate(flops=cost, bytes_accessed=cost, transcendentals=0),
    )


def shaped(*shape, dtype=F32):
    return jax.ShapeDtypeStruct(shape, dtype)


def local(members, groups, fine_state, coarse_boxes, piece_owner, piece_box):
    y_cells = fine_state.shape[1]
    x_cells = fine_state.shape[2] // PS
    boxes = coarse_boxes.shape[0]
    pieces = piece_box.shape[0]
    capacity = max(4, 2 * pieces // members)
    slots = members * capacity
    chunks = x_cells * PS // LANES
    blocks = y_cells // ROWS
    patch_y = y_cells // PS
    assert chunks == PS and boxes == LANES and slots <= LANES and PS == QS
    assert y_cells == 4 * ROWS and pieces == SIDES * patch_y * (x_cells // PS)
    edge_rows = 2 * chunks
    rows_all = NF * QUANT * CF
    wide = SIDES * patch_y * LANES
    count = pltpu.SMEM((members,), I32)
    piece_list = pltpu.SMEM((pieces,), I32)
    dma = pltpu.SemaphoreType.DMA
    fine_shape = fine_state.shape
    vmem = lambda *shape: pltpu.VMEM(shape, F32)
    owners = piece_owner.reshape(pieces)

    msg_shape = (members, (NF + 1) * ROWS, LANES)
    edge_shape = (NF, edge_rows, LANES)
    msg, low_edge, high_edge, code = call(
        functools.partial(prep_kernel, members, capacity, boxes),
        "prep",
        (HB, HB, HB),
        [
            shaped(*msg_shape), shaped(*edge_shape), shaped(*edge_shape),
            shaped(SIDES * patch_y, ROWS, LANES, dtype=I32),
        ],
        (HB, HB, HB, VM),
        [
            piece_list, piece_list, count,
            vmem(NF, ROWS, fine_shape[2]), vmem(NF, ROWS, fine_shape[2]),
            vmem(NF, y_cells, LANES), vmem(NF, y_cells, LANES),
            vmem(*msg_shape), vmem(*edge_shape), vmem(*edge_shape),
            dma((6,)), dma((3,)),
        ],
        cost=1 << 18,
        limit=LIMITS[0],
    )(owners, piece_box, fine_state)
    got = lax.all_to_all(msg, "dev", split_axis=0, concat_axis=0, tiled=True)
    up = [(g, (g + 1) % groups) for g in range(groups)]
    down = [(b, a) for a, b in up]
    y_low = lax.ppermute(high_edge, "group", up)
    y_high = lax.ppermute(low_edge, "group", down)

    wz, table = call(
        build_kernel,
        "build",
        (VM, HB),
        [shaped(NF, PS, y_cells, LANES), shaped(TABLE_PAD, SIDES * boxes)],
        (VM, VM),
        [
            vmem(NF, chunks, ROWS, LANES),
            vmem(NF, boxes, CB * CB * CB),
            vmem(NF, CB * CB * CB, boxes),
            dma((NF,)),
        ],
        cost=1 << 23,
        limit=LIMITS[1],
    )(fine_state, coarse_boxes.transpose(1, 0, 2))

    got, y_low, y_high = lax.optimization_barrier((got, y_low, y_high))
    payload, hot_box = call(
        serve_kernel,
        "serve",
        (VM, VM),
        [shaped(slots, TABLE_PAD), shaped(slots, SIDES * boxes, dtype=BF16)],
        (HB, VM),
        [vmem(slots, TABLE_PAD), dma((1,))],
        cost=1 << 18,
        limit=LIMITS[2],
    )(got, table)
    back = lax.all_to_all(payload, "dev", split_axis=0, concat_axis=0, tiled=True)

    (plane,) = call(
        functools.partial(plane_kernel, members),
        "plane",
        (VM, VM, VM, VM, VM),
        [shaped(NF, chunks, y_cells, LANES)],
        (VM,),
        [vmem(NF, chunks, y_cells, LANES)],
        cost=1 << 24,
        limit=LIMITS[3],
    )(got, y_low, y_high, fine_state, hot_box)

    terms, edge = call(
        functools.partial(face_kernel, slots),
        "face",
        (VM, VM, VM, VM),
        [shaped(slots, LANES), shaped(NF, 4, y_cells, LANES)],
        (HB, VM),
        [
            pltpu.VMEM((CF * slots, wide), BF16),
            vmem(TABLE_PAD, slots),
            vmem(rows_all, CF * slots),
            vmem(rows_all, wide),
            vmem(SIDES, NF, y_cells, LANES),
            vmem(TERM_ROWS, wide),
            vmem(slots, LANES),
            dma((1,)),
        ],
        cost=1 << 20,
        limit=LIMITS[4],
    )(back, code, wz, plane)
    incoming = lax.all_to_all(terms, "dev", split_axis=0, concat_axis=0, tiled=True)

    (fine_next,) = call(
        final_kernel,
        "final",
        (VM, VM, VM),
        [shaped(*fine_shape)],
        (HB,),
        [vmem(NF, PS - 2, ROWS, LANES), vmem(*fine_shape), dma((blocks,))],
        cost=1 << 23,
        limit=LIMITS[5],
    )(wz, plane, edge)
    (flux_register,) = call(
        register_kernel,
        "register",
        (VM, VM),
        [shaped(NF, SIDES * CF * CF, boxes)],
        (VM,),
        [vmem(LANES, SIDES * boxes)],
        cost=1 << 18,
        limit=LIMITS[6],
    )(incoming, hot_box)
    return (fine_next, flux_register)


def solution(mesh):
    in_specs = (
        P(None, "group", "dev"),
        P(("group", "dev"), None, None),
        P(("group", "dev"), None),
        P(("group", "dev")),
    )
    out_specs = (P(None, "group", "dev"), P(None, None, ("group", "dev")))
    body = functools.partial(local, mesh.shape["dev"], mesh.shape["group"])
    return jax.shard_map(body, mesh=mesh, in_specs=in_specs, out_specs=out_specs, check_vma=False)
```

```python
import functools

import jax
import jax.numpy as jnp
from jax import lax
from jax.experimental import pallas as pl
from jax.experimental.pallas import tpu as pltpu
from jax.sharding import PartitionSpec as P


PS = 16
RATIO = 4
QS = 16
CF = 4
CB = 8
NF = 5
LANES = 128
ROWS = 8
SIDES = 2
QUANT = 4

GAMMA = 1.4
DT_DX = 0.08
OFFSETS = [(i + 0.5) / RATIO - 0.5 for i in range(RATIO)]
F32, BF16, I32 = jnp.float32, jnp.bfloat16, jnp.int32
TABLE_ROWS = NF * QUANT * CF * CF
TABLE_PAD = 384
TERM_ROWS = 32
Y_EARLY = 1
NEAR = 3


def iota(shape, dim):
    return lax.broadcasted_iota(I32, shape, dim)


def minmod(a, b):
    return jnp.maximum(jnp.minimum(a, b), 0.0) + jnp.minimum(jnp.maximum(a, b), 0.0)


def to_primitive(cons):
    inverse = 1.0 / cons[0]
    velocity = [cons[1 + i] * inverse for i in range(3)]
    kinetic = cons[1] * velocity[0] + cons[2] * velocity[1] + cons[3] * velocity[2]
    return [cons[0]] + velocity + [(GAMMA - 1.0) * (cons[4] - 0.5 * kinetic)]


def hll(low, up, normal):
    others = [1 + i for i in range(3) if i != normal]
    u_low, u_up = low[1 + normal], up[1 + normal]
    p_low, p_up = low[4], up[4]
    g_low, g_up = GAMMA * p_low, GAMMA * p_up
    c_low = g_low * lax.rsqrt(g_low * low[0])
    c_up = g_up * lax.rsqrt(g_up * up[0])
    slow = jnp.minimum(jnp.minimum(u_low - c_low, u_up - c_up), 0.0)
    fast = jnp.maximum(jnp.maximum(u_low + c_low, u_up + c_up), 0.0)
    inverse = 1.0 / (fast - slow)
    f = fast * inverse
    s = slow * inverse
    a = f * (u_low - slow)
    b = s * (u_up - fast)
    m_low = a * low[0]
    m_up = b * up[0]
    k_low = 0.5 * (low[1] * low[1] + low[2] * low[2] + low[3] * low[3])
    k_up = 0.5 * (up[1] * up[1] + up[2] * up[2] + up[3] * up[3])
    rest = 1.0 / (GAMMA - 1.0)
    flux = [m_low - m_up, None, None, None, None]
    for i in others:
        flux[i] = m_low * low[i] - m_up * up[i]
    flux[1 + normal] = (m_low * u_low + f * p_low) - (m_up * u_up + s * p_up)
    flux[4] = (m_low * k_low + p_low * (rest * a + f * u_low)) - (
        m_up * k_up + p_up * (rest * b + s * u_up)
    )
    return flux


def split3(x):
    high = x.astype(BF16)
    left = x - high.astype(F32)
    middle = left.astype(BF16)
    low = (left - middle.astype(F32)).astype(BF16)
    return [high, middle, low]


def swap_groups(tiles, lane):
    tiles = list(tiles)
    bit = 0
    while (1 << bit) < len(tiles):
        step = 1 << bit
        upper = ((lane >> bit) & 1) == 1
        for i in range(len(tiles)):
            if not i & step:
                first, second = tiles[i], tiles[i + step]
                tiles[i] = jnp.where(upper, pltpu.roll(second, step, 1), first)
                tiles[i + step] = jnp.where(upper, second, pltpu.roll(first, LANES - step, 1))
        bit += 1
    return tiles


def count_slots(owner_ref, count_ref, members, capacity, pieces):
    for m in range(members):
        count_ref[m] = 0
    slots = []
    for p in range(pieces):
        owner = owner_ref[p]
        rank = count_ref[owner]
        count_ref[owner] = rank + 1
        slots.append(owner * capacity + rank)
    return slots


def prep_kernel(
    members, capacity, boxes, owner_hbm, box_hbm, fine_hbm, msg_hbm, lo_hbm, hi_hbm, code_ref,
    owner_ref, box_ref, count_ref, low_ref, high_ref, left_ref, right_ref,
    msg_ref, lo_ref, hi_ref, sem_ref, out_sem,
):
    me = lax.axis_index("dev")
    pieces = box_hbm.shape[0]
    y_cells = fine_hbm.shape[1]
    chunks = fine_hbm.shape[2] // LANES
    blocks = y_cells // ROWS
    ends = [
        (owner_hbm, owner_ref),
        (box_hbm, box_ref),
        (fine_hbm.at[:, :, 0:LANES], left_ref),
        (fine_hbm.at[:, :, (chunks - 1) * LANES : chunks * LANES], right_ref),
        (fine_hbm.at[:, 0:ROWS, :], low_ref),
        (fine_hbm.at[:, y_cells - ROWS : y_cells, :], high_ref),
    ]
    copies = [pltpu.make_async_copy(a, b, sem_ref.at[i]) for i, (a, b) in enumerate(ends)]
    for copy in copies:
        copy.start()
    lane = iota((ROWS, LANES), 1)
    sub = iota((ROWS, LANES), 0)
    copies[0].wait()
    copies[1].wait()
    slots = count_slots(owner_ref, count_ref, members, capacity, pieces)
    values = jnp.zeros((ROWS, LANES), I32)
    for p in range(pieces):
        values = jnp.where(lane == slots[p], box_ref[p] + (boxes * (p % SIDES) + 1), values)
    values = jnp.where(sub == 0, values, 0).astype(F32)
    mine = (lane >= me * capacity) & (lane < (me + 1) * capacity)
    for m in range(members):
        shift = lax.rem((me - m) * capacity + LANES * members, LANES)
        msg_ref[m, NF * ROWS :, :] = jnp.where(mine, pltpu.roll(values, shift, 1), 0.0)
    width = 2 * PS
    copies[2].wait()
    copies[3].wait()
    for f in range(NF):
        left = left_ref[f, 0:ROWS, :]
        right = pltpu.roll(right_ref[f, 0:ROWS, :], width, 1)
        for g in range(1, blocks):
            rows = slice(g * ROWS, (g + 1) * ROWS)
            here = lane // width == g
            left = jnp.where(here, pltpu.roll(left_ref[f, rows, :], width * g, 1), left)
            edge = right_ref[f, rows, :]
            shift = (width * (g + 1)) % LANES
            right = jnp.where(here, pltpu.roll(edge, shift, 1) if shift else edge, right)
        for m in range(members):
            below = jnp.full((ROWS, LANES), m, I32) < me
            msg_ref[m, f * ROWS : (f + 1) * ROWS, :] = jnp.where(below, left, right)
    outs = [pltpu.make_async_copy(msg_ref, msg_hbm, out_sem.at[0])]
    outs[0].start()
    patch_y = y_cells // PS
    patch_x = chunks * LANES // PS // PS
    x_cell = (lane % PS) * (LANES // PS) + lane // PS
    for s in range(SIDES):
        for ky in range(patch_y):
            code = jnp.zeros((ROWS, LANES), I32)
            for kx in range(patch_x):
                slot = slots[(ky * patch_x + kx) * SIDES + s]
                code = jnp.where(x_cell // PS == kx, slot, code)
            code_ref[s * patch_y + ky] = code + (x_cell // RATIO) % CF * (members * capacity)
    copies[4].wait()
    copies[5].wait()
    for f in range(NF):
        for j in range(chunks // 4):
            low = high = None
            for k in range(4):
                c = slice((4 * j + k) * LANES, (4 * j + k + 1) * LANES)
                first = low_ref[f, :, c]
                last = high_ref[f, :, c]
                first = pltpu.roll(first, 2 * k, 0) if k else first
                last = pltpu.roll(last, 2 * k + 2, 0) if k < 3 else last
                low = first if k == 0 else jnp.where(sub // 2 == k, first, low)
                high = last if k == 0 else jnp.where(sub // 2 == k, last, high)
            lo_ref[f, j * ROWS : (j + 1) * ROWS, :] = low
            hi_ref[f, j * ROWS : (j + 1) * ROWS, :] = high
    outs.append(pltpu.make_async_copy(lo_ref, lo_hbm, out_sem.at[1]))
    outs.append(pltpu.make_async_copy(hi_ref, hi_hbm, out_sem.at[2]))
    outs[1].start()
    outs[2].start()
    for copy in outs:
        copy.wait()


def build_kernel(
    fine_ref, coarse_hbm, wz_hbm, tab_ref, wn_ref, wz_ref, cs_ref, ct_ref, coarse_sem, wz_sem
):
    chunks = fine_ref.shape[2] // LANES
    blocks = fine_ref.shape[1] // ROWS
    coarse_copies = [
        pltpu.make_async_copy(coarse_hbm.at[f], cs_ref.at[f], coarse_sem.at[f]) for f in range(NF)
    ]
    for copy in coarse_copies:
        copy.start()
    lane = iota((ROWS, LANES), 1)

    def turn(block, carry):
        rows = pl.ds(pl.multiple_of(block * ROWS, ROWS), ROWS)
        for c in range(chunks):
            prim = to_primitive(
                [fine_ref[f, rows, c * LANES : (c + 1) * LANES] for f in range(NF)]
            )
            for f in range(NF):
                wn_ref[f, c] = prim[f]
        for f in range(NF):
            tiles = swap_groups([wn_ref[f, c] for c in range(chunks)], lane)
            for z in range(PS):
                wz_ref[f, z, rows, :] = tiles[z]
        return carry

    lax.fori_loop(0, blocks, turn, 0)
    wz_copy = pltpu.make_async_copy(wz_ref, wz_hbm, wz_sem.at[0])
    wz_copy.start()
    sub = iota((ROWS, LANES), 0)
    boxes = coarse_hbm.shape[1]
    for f in range(NF):
        coarse_copies[f].wait()
        for j in range(CB * CB * CB // LANES):
            at = slice(j * LANES, (j + 1) * LANES)
            ct_ref[f, at, :] = cs_ref[f, :, at].T
    for s in range(SIDES):
        middle = CB - 3 if s == 0 else 2

        def cells(z, y):
            at = (z * CB + y) * CB
            return to_primitive([ct_ref[f, at : at + CB, :] for f in range(NF)])

        centre = {y: cells(middle, y) for y in range(1, CB - 1)}
        found = {}
        for cy in range(CF):
            y = cy + 2
            below, above = cells(middle - 1, y), cells(middle + 1, y)
            for f in range(NF):
                c = centre[y][f]
                found[f, 0, cy] = c
                found[f, 1, cy] = minmod(c - below[f], above[f] - c)
                found[f, 2, cy] = minmod(c - centre[y - 1][f], centre[y + 1][f] - c)
                found[f, 3, cy] = minmod(c - pltpu.roll(c, 1, 0), pltpu.roll(c, ROWS - 1, 0) - c)
        for f in range(NF):
            for q in range(QUANT):
                at = (f * QUANT + q) * CF * CF
                for i in range(2):
                    tab_ref[at + i * ROWS : at + (i + 1) * ROWS, s * boxes : (s + 1) * boxes] = (
                        jnp.where(
                            sub < CF,
                            pltpu.roll(found[f, q, 2 * i], ROWS - 2, 0),
                            pltpu.roll(found[f, q, 2 * i + 1], 2, 0),
                        )
                    )
    wz_copy.wait()


def serve_kernel(msg_ref, tab_ref, out_hbm, hot_ref, out_ref, sem_ref):
    members = msg_ref.shape[0]
    slot_count = out_ref.shape[0]
    row = msg_ref[0, NF * ROWS :, :]
    for m in range(1, members):
        row = row + msg_ref[m, NF * ROWS :, :]
    shape = (slot_count, LANES)
    wide = jnp.broadcast_to(row[0:1, :], shape)
    column = jnp.sum(jnp.where(iota(shape, 0) == iota(shape, 1), wide, 0.0), axis=1, keepdims=True)
    target = column.astype(I32) - 1
    hot = jnp.where(iota(hot_ref.shape, 1) == target, 1.0, 0.0).astype(BF16)
    hot_ref[...] = hot
    total = None
    for part in split3(tab_ref[...]):
        got = lax.dot_general(
            hot, part, (((1,), (1,)), ((), ())), preferred_element_type=F32
        )
        total = got if total is None else total + got
    out_ref[:, 0:TABLE_ROWS] = total
    out_ref[:, TABLE_ROWS:] = jnp.zeros((slot_count, TABLE_PAD - TABLE_ROWS), F32)
    copy = pltpu.make_async_copy(out_ref, out_hbm, sem_ref.at[0])
    copy.start()
    copy.wait()


def sweep_line(tiles, normal, back, forward, emit, finish=None):
    fields = range(NF)
    last = len(tiles) - 1
    moved = [[back(None, t[f]) for f in fields] for t in tiles]
    diff = [
        [t[f] - back(moved[max(i - 1, 0)][f], moved[i][f]) for f in fields]
        for i, t in enumerate(tiles)
    ]
    diff_moved = [[forward(None, d[f]) for f in fields] for d in diff]
    low_moved = None
    flux = flux_moved = None
    for i, t in enumerate(tiles):
        half = [
            0.5 * minmod(diff[i][f], forward(diff_moved[i][f], diff_moved[min(i + 1, last)][f]))
            for f in fields
        ]
        if i == last and finish is not None:
            finish(low_moved, [t[f] - half[f] for f in fields], flux, flux_moved)
            return
        low_next = [back(None, t[f] + half[f]) for f in fields]
        if i > 0:
            left = [back(low_moved[f], low_next[f]) for f in fields]
            new = hll(left, [t[f] - half[f] for f in fields], normal)
            new_moved = [forward(None, new[f]) for f in fields]
            if i > 1:
                emit(i - 2, [forward(flux_moved[f], new_moved[f]) - flux[f] for f in fields])
            flux, flux_moved = new, new_moved
        low_moved = low_next


def y_columns(j, skip, blocks, lo_ref, hi_ref, load, add):
    sub = iota((ROWS, LANES), 0)

    def y_back(before, here):
        if before is None:
            return pltpu.roll(here, 1, 0)
        return jnp.where(sub < 1, before, here)

    def y_forward(here, after):
        if here is None:
            return pltpu.roll(after, ROWS - 1, 0)
        return jnp.where(sub >= ROWS - 1, after, here)

    ends = []
    for k in range(ROWS):
        at = slice((2 * (j - skip) + k // 4) * ROWS, (2 * (j - skip) + k // 4 + 1) * ROWS)
        if k % 4 == 0:
            low = to_primitive([lo_ref[f, at, :] for f in range(NF)])
            high = to_primitive([hi_ref[f, at, :] for f in range(NF)])
        c = ROWS * j + k
        turn_low, turn_high = (6 - 2 * (k % 4)) % ROWS, (ROWS - 2 * (k % 4)) % ROWS
        below = [pltpu.roll(t, turn_low, 0) if turn_low else t for t in low]
        above = [pltpu.roll(t, turn_high, 0) if turn_high else t for t in high]
        tiles = [load(c, b) for b in range(blocks)]

        def emit(b, change):
            for f in range(NF):
                add(f, c, b, change[f])

        sweep_line(
            [below] + tiles + [above], 1, y_back, y_forward, emit, lambda *end: ends.append(end)
        )
    packed = []
    for which in range(2):
        state = []
        for f in range(NF):
            tile = ends[0][which][f]
            for k in range(1, ROWS):
                tile = jnp.where(sub == k, pltpu.roll(ends[k][which][f], k, 0), tile)
            state.append(tile)
        packed.append(state)
    top = hll(packed[0], packed[1], 1)
    for k in range(ROWS):
        c = ROWS * j + k
        flux, flux_moved = ends[k][2], ends[k][3]
        for f in range(NF):
            moved = pltpu.roll(top[f], ROWS - 1 - k, 0) if k < ROWS - 1 else top[f]
            change = y_forward(flux_moved[f], moved) - flux[f]
            add(f, c, blocks - 1, change)


def plane_kernel(
    members, msg_ref, lo_ref, hi_ref, fine_ref, after_ref, wz_hbm,
    out_ref, near_ref, ends_ref, wn_ref, sem_ref,
):
    near_copies = [
        pltpu.make_async_copy(
            wz_hbm.at[:, start : start + NEAR],
            near_ref.at[:, i * NEAR : (i + 1) * NEAR],
            sem_ref.at[i],
        )
        for i, start in enumerate((0, PS - NEAR))
    ]
    for copy in near_copies:
        copy.start()
    me = lax.axis_index("dev")
    chunks = fine_ref.shape[2] // LANES
    blocks = fine_ref.shape[1] // ROWS
    lane = iota((ROWS, LANES), 1)
    width = 2 * PS
    place = jnp.full((ROWS, LANES), me, I32)

    def x_back(before, here):
        if before is None:
            return pltpu.roll(here, PS, 1)
        return jnp.where(lane < PS, before, here)

    def x_forward(here, after):
        if here is None:
            return pltpu.roll(after, LANES - PS, 1)
        return jnp.where(lane >= LANES - PS, after, here)

    def x_block(block, carry):
        rows = pl.ds(pl.multiple_of(block * ROWS, ROWS), ROWS)
        left = jnp.maximum(me - 1, 0)
        right = jnp.minimum(me + 1, members - 1)
        shift_low = lax.rem(2 * LANES - width - width * block, LANES)
        shift_high = lax.rem(LANES - width * block, LANES)
        low = to_primitive(
            [pltpu.roll(msg_ref[left, f * ROWS : (f + 1) * ROWS, :], shift_low, 1) for f in range(NF)]
        )
        high = to_primitive(
            [pltpu.roll(msg_ref[right, f * ROWS : (f + 1) * ROWS, :], shift_high, 1) for f in range(NF)]
        )
        tiles = []
        for c in range(chunks):
            prim = to_primitive(
                [fine_ref[f, rows, c * LANES : (c + 1) * LANES] for f in range(NF)]
            )
            for f in range(NF):
                wn_ref[f, c, rows, :] = prim[f]
            tiles.append(prim)
        for f in range(NF):
            w = tiles[0][f]
            same = jnp.where(
                lane < LANES - PS, pltpu.roll(w, LANES - width, 1), pltpu.roll(w, LANES - PS, 1)
            )
            low[f] = jnp.where(place == 0, same, low[f])
            w = tiles[-1][f]
            same = jnp.where(lane < PS, pltpu.roll(w, PS, 1), pltpu.roll(w, width, 1))
            high[f] = jnp.where(place == members - 1, same, high[f])

        def emit(c, change):
            at = slice(c * LANES, (c + 1) * LANES)
            for f in range(NF):
                out_ref[f, c, rows, :] = fine_ref[f, rows, at] - DT_DX * change[f]

        sweep_line([low] + tiles + [high], 0, x_back, x_forward, emit)
        return carry

    lax.fori_loop(0, blocks, x_block, 0)

    def load(c, b):
        return [wn_ref[f, c, b * ROWS : (b + 1) * ROWS, :] for f in range(NF)]

    def add(f, c, b, change):
        at = slice(b * ROWS, (b + 1) * ROWS)
        out_ref[f, c, at, :] = out_ref[f, c, at, :] - DT_DX * change

    first = 2 * ROWS * Y_EARLY
    ends_ref[0] = lo_ref[:, first:, :]
    ends_ref[1] = hi_ref[:, first:, :]
    for j in range(Y_EARLY):
        y_columns(j, 0, blocks, lo_ref, hi_ref, load, add)
    for copy in near_copies:
        copy.wait()


def face_kernel(
    slot_count, got_ref, code_ref, near_ref, after_ref, term_hbm, edge_hbm,
    edge_ref, he_ref, rt_ref, lf_ref, g_ref, fs_ref, v_ref, term_ref, sem_ref,
):
    lane = iota((ROWS, LANES), 1)
    sub = iota((ROWS, LANES), 0)
    rows_all = NF * QUANT * CF
    y_cells = near_ref.shape[2]
    blocks = y_cells // ROWS
    patch_y = y_cells // PS
    number = iota((CF * slot_count, LANES), 0)
    for i in range(code_ref.shape[0]):
        hot = jnp.where(number == code_ref[i, 0:1, :], 1.0, 0.0)
        he_ref[:, i * LANES : (i + 1) * LANES] = hot.astype(BF16)
    rt_ref[...] = got_ref[...].T
    for cx in range(CF):
        lf_ref[:, cx * slot_count : (cx + 1) * slot_count] = rt_ref[
            pl.ds(cx, rows_all, stride=CF), :
        ]
    parts = jnp.concatenate(split3(lf_ref[...]), axis=0)
    product = jnp.dot(parts, he_ref[...], preferred_element_type=F32)
    g_ref[...] = (
        product[0:rows_all] + product[rows_all : 2 * rows_all] + product[2 * rows_all :]
    )

    def pick(options, index):
        value = jnp.full((ROWS, LANES), options[0], F32)
        for i in range(1, RATIO):
            value = jnp.where(index == i, options[i], value)
        return value

    off_y = pick(OFFSETS, sub % RATIO)
    off_x = pick(OFFSETS, (lane // PS) % RATIO)
    for block in range(blocks):
        ky, half = block // (blocks // patch_y), block % (blocks // patch_y)
        rows = slice(block * ROWS, (block + 1) * ROWS)
        for s in range(SIDES):
            at = (s * patch_y + ky) * LANES
            ghosts = [[], []]
            for f in range(NF):
                terms = []
                for q in range(QUANT):
                    r = (f * QUANT + q) * CF + 2 * half
                    terms.append(
                        jnp.where(
                            sub < RATIO,
                            jnp.broadcast_to(g_ref[r : r + 1, at : at + LANES], (ROWS, LANES)),
                            jnp.broadcast_to(g_ref[r + 1 : r + 2, at : at + LANES], (ROWS, LANES)),
                        )
                    )
                for i in range(2):
                    off_z = OFFSETS[i + (RATIO - 2 if s == 0 else 0)]
                    ghosts[i].append(
                        ((terms[0] + terms[1] * off_z) + terms[2] * off_y) + terms[3] * off_x
                    )

            inner = [
                [near_ref[f, NEAR * s + i, rows, :] for f in range(NF)] for i in range(NEAR)
            ]
            line = ghosts + inner if s == 0 else inner + ghosts
            diff = [[line[i + 1][f] - line[i][f] for f in range(NF)] for i in range(4)]
            half_slope = [
                [0.5 * minmod(diff[i][f], diff[i + 1][f]) for f in range(NF)] for i in range(3)
            ]
            flux = [
                hll(
                    [line[i + 1][f] + half_slope[i][f] for f in range(NF)],
                    [line[i + 2][f] - half_slope[i + 1][f] for f in range(NF)],
                    2,
                )
                for i in range(2)
            ]
            for f in range(NF):
                if s == 0:
                    edge_ref[f, 0, rows, :] = flux[1][f] - flux[0][f]
                    edge_ref[f, 1, rows, :] = -flux[1][f]
                    fs_ref[0, f, rows, :] = flux[0][f]
                else:
                    edge_ref[f, 2, rows, :] = flux[0][f]
                    edge_ref[f, 3, rows, :] = flux[1][f] - flux[0][f]
                    fs_ref[1, f, rows, :] = flux[1][f]

    edge_copy = pltpu.make_async_copy(edge_ref, edge_hbm, sem_ref.at[1])
    edge_copy.start()
    v_ref[NF * CF :, :] = jnp.zeros((TERM_ROWS - NF * CF, v_ref.shape[1]), F32)
    for s in range(SIDES):
        for f in range(NF):
            total = None
            for i in range(RATIO):
                got = fs_ref[s, f, pl.ds(i, y_cells // RATIO, stride=RATIO), :]
                total = got if total is None else total + got
            total = total * (1.0 / RATIO)
            for ky in range(patch_y):
                at = (s * patch_y + ky) * LANES
                v_ref[f * CF : (f + 1) * CF, at : at + LANES] = total[ky * CF : (ky + 1) * CF]
    parts = jnp.concatenate(split3(v_ref[...]), axis=0)
    product = lax.dot_general(
        parts, he_ref[...], (((1,), (1,)), ((), ())), preferred_element_type=F32
    )
    summed = (
        product[0:TERM_ROWS] + product[TERM_ROWS : 2 * TERM_ROWS] + product[2 * TERM_ROWS :]
    )
    turned = summed.T
    for cx in range(CF):
        term_ref[:, cx * TERM_ROWS : (cx + 1) * TERM_ROWS] = turned[
            cx * slot_count : (cx + 1) * slot_count, :
        ]
    copy = pltpu.make_async_copy(term_ref, term_hbm, sem_ref.at[0])
    copy.start()
    edge_copy.wait()
    copy.wait()


def final_kernel(
    fine_ref, plane_ref, edge_hbm, ends_ref, wz_hbm, out_hbm,
    edge_ref, wz_ref, zc_ref, extra_ref, out_ref, wz_sem, out_sem,
):
    lane = iota((ROWS, LANES), 1)
    chunks = plane_ref.shape[1]
    blocks = plane_ref.shape[2] // ROWS

    def wz_copy(block):
        rows = pl.ds(pl.multiple_of(block * ROWS, ROWS), ROWS)
        return pltpu.make_async_copy(
            wz_hbm.at[:, :, rows, :], wz_ref.at[:, :, rows, :], wz_sem.at[block]
        )

    def out_copy(block):
        rows = pl.ds(pl.multiple_of(block * ROWS, ROWS), ROWS)
        return pltpu.make_async_copy(
            out_ref.at[:, rows, :], out_hbm.at[:, rows, :], out_sem.at[block]
        )

    edge_copy = pltpu.make_async_copy(edge_hbm, edge_ref, wz_sem.at[blocks])
    edge_copy.start()
    for block in range(blocks):
        wz_copy(block).start()
    first = Y_EARLY * ROWS

    def load(c, b):
        at = slice(b * ROWS, (b + 1) * ROWS)
        return to_primitive([fine_ref[f, at, c * LANES : (c + 1) * LANES] for f in range(NF)])

    def add(f, c, b, change):
        at = slice(b * ROWS, (b + 1) * ROWS)
        extra_ref[f, c - first, at, :] = plane_ref[f, c, at, :] - DT_DX * change

    for j in range(Y_EARLY, chunks // ROWS):
        y_columns(j, Y_EARLY, blocks, ends_ref.at[0], ends_ref.at[1], load, add)

    edge_copy.wait()

    def step(block, carry):
        rows = pl.ds(pl.multiple_of(block * ROWS, ROWS), ROWS)
        wz_copy(block).wait()

        def load(z):
            return [wz_ref[f, z, rows, :] for f in range(NF)]

        w_here = load(1)
        w_before = load(0)
        diff = [w_here[f] - w_before[f] for f in range(NF)]
        low = flux = None
        for z in range(1, PS - 1):
            w_next = load(z + 1)
            diff_next = [w_next[f] - w_here[f] for f in range(NF)]
            half = [0.5 * minmod(diff[f], diff_next[f]) for f in range(NF)]
            if z >= 2:
                new = hll(low, [w_here[f] - half[f] for f in range(NF)], 2)
                for f in range(NF):
                    before = edge_ref[f, 1, rows, :] if z == 2 else -flux[f]
                    zc_ref[f, z - 2] = new[f] + before
                flux = new
            low = [w_here[f] + half[f] for f in range(NF)]
            w_here, diff = w_next, diff_next
        for f in range(NF):
            zc_ref[f, PS - 3] = edge_ref[f, 2, rows, :] - flux[f]
        for f in range(NF):
            tiles = [edge_ref[f, 0, rows, :]]
            tiles += [zc_ref[f, z] for z in range(PS - 2)]
            tiles += [edge_ref[f, 3, rows, :]]
            tiles = swap_groups(tiles, lane)
            for c in range(chunks):
                at = slice(c * LANES, (c + 1) * LANES)
                if c < first:
                    partial = plane_ref[f, c, rows, :]
                else:
                    partial = extra_ref[f, c - first, rows, :]
                out_ref[f, rows, at] = partial - DT_DX * tiles[c]
        out_copy(block).start()
        return carry

    lax.fori_loop(0, blocks, step, 0)

    for block in range(blocks):
        out_copy(block).wait()


def register_kernel(got_ref, hot_ref, out_ref, z_ref):
    boxes = out_ref.shape[2]
    turned = got_ref[...].T
    parts = jnp.concatenate(split3(turned), axis=0)
    product = jnp.dot(parts, hot_ref[...], preferred_element_type=F32)
    z_ref[...] = product[0:LANES] + product[LANES : 2 * LANES] + product[2 * LANES :]
    for f in range(NF):
        for cx in range(CF):
            at = cx * TERM_ROWS + f * CF
            for s in range(SIDES):
                out_ref[f, pl.ds(s * CF * CF + cx, CF, stride=CF), :] = z_ref[
                    at : at + CF, s * boxes : (s + 1) * boxes
                ]


VM = pl.BlockSpec(memory_space=pltpu.VMEM)
HB = pl.BlockSpec(memory_space=pltpu.HBM)


def call(body, ins, outs, out_specs, scratch=(), cost=0, limit=8 << 10):
    kernel = pl.pallas_call(
        body,
        in_specs=list(ins),
        out_specs=list(out_specs),
        out_shape=[
            pltpu.HBM(o.shape, o.dtype) if spec is HB else o for o, spec in zip(outs, out_specs)
        ],
        scratch_shapes=list(scratch),
        compiler_params=pltpu.CompilerParams(vmem_limit_bytes=limit << 10),
        cost_estimate=pl.CostEstimate(flops=cost, bytes_accessed=cost, transcendentals=0),
    )

    def run(*args):
        return kernel(
            *[
                pltpu.with_memory_space_constraint(a, pltpu.HBM) if spec is HB else a
                for a, spec in zip(args, ins)
            ]
        )

    return run


def shaped(*shape, dtype=F32):
    return jax.ShapeDtypeStruct(shape, dtype)


def local(members, groups, fine_state, coarse_boxes, piece_owner, piece_box):
    y_cells = fine_state.shape[1]
    x_cells = fine_state.shape[2] // PS
    boxes = coarse_boxes.shape[0]
    pieces = piece_box.shape[0]
    capacity = max(4, 2 * pieces // members)
    slots = members * capacity
    chunks = x_cells * PS // LANES
    blocks = y_cells // ROWS
    patch_y = y_cells // PS
    assert chunks == PS and boxes == LANES and slots <= LANES and PS == QS
    assert y_cells == 4 * ROWS and pieces == SIDES * patch_y * (x_cells // PS)
    edge_rows = 2 * chunks
    rows_all = NF * QUANT * CF
    wide = SIDES * patch_y * LANES
    count = pltpu.SMEM((members,), I32)
    piece_list = pltpu.SMEM((pieces,), I32)
    dma = pltpu.SemaphoreType.DMA
    fine_shape = fine_state.shape
    vmem = lambda *shape: pltpu.VMEM(shape, F32)
    owners = piece_owner.reshape(pieces)

    msg_shape = (members, (NF + 1) * ROWS, LANES)
    edge_shape = (NF, edge_rows, LANES)
    msg, low_edge, high_edge, code = call(
        functools.partial(prep_kernel, members, capacity, boxes),
        (HB, HB, HB),
        [
            shaped(*msg_shape), shaped(*edge_shape), shaped(*edge_shape),
            shaped(SIDES * patch_y, ROWS, LANES, dtype=I32),
        ],
        (HB, HB, HB, VM),
        [
            piece_list, piece_list, count,
            vmem(NF, ROWS, fine_shape[2]), vmem(NF, ROWS, fine_shape[2]),
            vmem(NF, y_cells, LANES), vmem(NF, y_cells, LANES),
            vmem(*msg_shape), vmem(*edge_shape), vmem(*edge_shape),
            dma((6,)), dma((3,)),
        ],
        cost=1 << 18,
    )(owners, piece_box, fine_state)
    got = lax.all_to_all(msg, "dev", split_axis=0, concat_axis=0, tiled=True)
    up = [(g, (g + 1) % groups) for g in range(groups)]
    down = [(b, a) for a, b in up]
    y_low = lax.ppermute(high_edge, "group", up)
    y_high = lax.ppermute(low_edge, "group", down)

    turned_shape = (NF, PS, y_cells, LANES)
    build = call(
        build_kernel,
        (VM, HB),
        [
            shaped(*turned_shape),
            shaped(TABLE_ROWS, SIDES * boxes),
        ],
        (HB, VM),
        [
            vmem(NF, chunks, ROWS, LANES),
            vmem(*turned_shape),
            vmem(NF, boxes, CB * CB * CB),
            vmem(NF, CB * CB * CB, boxes),
            dma((NF,)),
            dma((1,)),
        ],
        cost=1 << 23,
    )
    wz, table = build(fine_state, coarse_boxes.transpose(1, 0, 2))
    payload, hot_box = call(
        serve_kernel,
        (VM, VM),
        [shaped(slots, TABLE_PAD), shaped(slots, SIDES * boxes, dtype=BF16)],
        (HB, VM),
        [vmem(slots, TABLE_PAD), dma((1,))],
        cost=1 << 18,
    )(got, table)
    back = lax.all_to_all(payload, "dev", split_axis=0, concat_axis=0, tiled=True)

    plane, near, ends = call(
        functools.partial(plane_kernel, members),
        (VM, VM, VM, VM, VM, HB),
        [
            shaped(NF, chunks, y_cells, LANES),
            shaped(NF, 2 * NEAR, y_cells, LANES),
            shaped(2, NF, edge_rows - 2 * ROWS * Y_EARLY, LANES),
        ],
        (VM, VM, VM),
        [
            vmem(NF, chunks, y_cells, LANES),
            dma((2,)),
        ],
        cost=1 << 24,
    )(got, y_low, y_high, fine_state, hot_box, wz)

    terms, edge = call(
        functools.partial(face_kernel, slots),
        (VM, VM, VM, VM),
        [shaped(slots, LANES), shaped(NF, 4, y_cells, LANES)],
        (HB, HB),
        [
            vmem(NF, 4, y_cells, LANES),
            pltpu.VMEM((CF * slots, wide), BF16),
            vmem(TABLE_PAD, slots),
            vmem(rows_all, CF * slots),
            vmem(rows_all, wide),
            vmem(SIDES, NF, y_cells, LANES),
            vmem(TERM_ROWS, wide),
            vmem(slots, LANES),
            dma((2,)),
        ],
        cost=1 << 20,
    )(back, code, near, plane)
    incoming = lax.all_to_all(terms, "dev", split_axis=0, concat_axis=0, tiled=True)

    (fine_next,) = call(
        final_kernel,
        (VM, VM, HB, VM, HB),
        [shaped(*fine_shape)],
        (HB,),
        [
            vmem(NF, 4, y_cells, LANES),
            vmem(*turned_shape),
            vmem(NF, PS - 2, ROWS, LANES),
            vmem(NF, chunks - Y_EARLY * ROWS, y_cells, LANES),
            vmem(*fine_shape),
            dma((blocks + 1,)),
            dma((blocks,)),
        ],
        cost=1 << 24,
    )(fine_state, plane, edge, ends, wz)
    (flux_register,) = call(
        register_kernel,
        (VM, VM),
        [shaped(NF, SIDES * CF * CF, boxes)],
        (VM,),
        [vmem(LANES, SIDES * boxes)],
        cost=1 << 18,
    )(incoming, hot_box)
    return (fine_next, flux_register)


def solution(mesh):
    in_specs = (
        P(None, "group", "dev"),
        P(("group", "dev"), None, None),
        P(("group", "dev"), None),
        P(("group", "dev")),
    )
    out_specs = (P(None, "group", "dev"), P(None, None, ("group", "dev")))
    body = functools.partial(local, mesh.shape["dev"], mesh.shape["group"])
    return jax.shard_map(body, mesh=mesh, in_specs=in_specs, out_specs=out_specs, check_vma=False)
```

```python
import functools

import jax
import jax.numpy as jnp
from jax import lax
from jax.experimental import pallas as pl
from jax.experimental.pallas import tpu as pltpu
from jax.sharding import PartitionSpec as P


PS = 16
RATIO = 4
QS = 16
CF = 4
CB = 8
NF = 5
LANES = 128
ROWS = 8
SIDES = 2
QUANT = 4

GAMMA = 1.4
DT_DX = 0.08
OFFSETS = [(i + 0.5) / RATIO - 0.5 for i in range(RATIO)]
F32, BF16, I32 = jnp.float32, jnp.bfloat16, jnp.int32
TABLE_ROWS = NF * QUANT * CF * CF
TABLE_PAD = 384
TERM_ROWS = 32
Y_EARLY = 8
NEAR = 3


def iota(shape, dim):
    return lax.broadcasted_iota(I32, shape, dim)


def minmod(a, b):
    return jnp.maximum(jnp.minimum(a, b), 0.0) + jnp.minimum(jnp.maximum(a, b), 0.0)


def to_primitive(cons):
    inverse = 1.0 / cons[0]
    velocity = [cons[1 + i] * inverse for i in range(3)]
    kinetic = cons[1] * velocity[0] + cons[2] * velocity[1] + cons[3] * velocity[2]
    return [cons[0]] + velocity + [(GAMMA - 1.0) * (cons[4] - 0.5 * kinetic)]


def hll(low, up, normal):
    others = [1 + i for i in range(3) if i != normal]
    u_low, u_up = low[1 + normal], up[1 + normal]
    p_low, p_up = low[4], up[4]
    g_low, g_up = GAMMA * p_low, GAMMA * p_up
    c_low = g_low * lax.rsqrt(g_low * low[0])
    c_up = g_up * lax.rsqrt(g_up * up[0])
    slow = jnp.minimum(jnp.minimum(u_low - c_low, u_up - c_up), 0.0)
    fast = jnp.maximum(jnp.maximum(u_low + c_low, u_up + c_up), 0.0)
    inverse = 1.0 / (fast - slow)
    f = fast * inverse
    s = slow * inverse
    a = f * (u_low - slow)
    b = s * (u_up - fast)
    m_low = a * low[0]
    m_up = b * up[0]
    k_low = 0.5 * (low[1] * low[1] + low[2] * low[2] + low[3] * low[3])
    k_up = 0.5 * (up[1] * up[1] + up[2] * up[2] + up[3] * up[3])
    rest = 1.0 / (GAMMA - 1.0)
    flux = [m_low - m_up, None, None, None, None]
    for i in others:
        flux[i] = m_low * low[i] - m_up * up[i]
    flux[1 + normal] = (m_low * u_low + f * p_low) - (m_up * u_up + s * p_up)
    flux[4] = (m_low * k_low + p_low * (rest * a + f * u_low)) - (
        m_up * k_up + p_up * (rest * b + s * u_up)
    )
    return flux


def split3(x):
    high = x.astype(BF16)
    left = x - high.astype(F32)
    middle = left.astype(BF16)
    low = (left - middle.astype(F32)).astype(BF16)
    return [high, middle, low]


def swap_groups(tiles, lane):
    count = len(tiles)
    tiles = [pltpu.roll(t, c, 1) if c else t for c, t in enumerate(tiles)]
    step = 1
    while step < count:
        odd = lane // step % 2 == 1
        tiles = [jnp.where(odd, tiles[(i + step) % count], tiles[i]) for i in range(count)]
        step *= 2
    return [
        pltpu.roll(tiles[count - z], LANES - z, 1) if z else tiles[0] for z in range(count)
    ]


def count_slots(owner_ref, count_ref, members, capacity, pieces):
    for m in range(members):
        count_ref[m] = 0
    slots = []
    for p in range(pieces):
        owner = owner_ref[p]
        rank = count_ref[owner]
        count_ref[owner] = rank + 1
        slots.append(owner * capacity + rank)
    return slots


def prep_kernel(
    members, capacity, boxes, owner_hbm, box_hbm, fine_hbm, msg_hbm, lo_hbm, hi_hbm, code_ref,
    owner_ref, box_ref, count_ref, low_ref, high_ref, left_ref, right_ref,
    msg_ref, lo_ref, hi_ref, sem_ref, out_sem,
):
    me = lax.axis_index("dev")
    pieces = box_hbm.shape[0]
    y_cells = fine_hbm.shape[1]
    chunks = fine_hbm.shape[2] // LANES
    blocks = y_cells // ROWS
    ends = [
        (owner_hbm, owner_ref),
        (box_hbm, box_ref),
        (fine_hbm.at[:, :, 0:LANES], left_ref),
        (fine_hbm.at[:, :, (chunks - 1) * LANES : chunks * LANES], right_ref),
        (fine_hbm.at[:, 0:ROWS, :], low_ref),
        (fine_hbm.at[:, y_cells - ROWS : y_cells, :], high_ref),
    ]
    copies = [pltpu.make_async_copy(a, b, sem_ref.at[i]) for i, (a, b) in enumerate(ends)]
    for copy in copies:
        copy.start()
    lane = iota((ROWS, LANES), 1)
    sub = iota((ROWS, LANES), 0)
    copies[0].wait()
    copies[1].wait()
    slots = count_slots(owner_ref, count_ref, members, capacity, pieces)
    values = jnp.zeros((ROWS, LANES), I32)
    for p in range(pieces):
        values = jnp.where(lane == slots[p], box_ref[p] + (boxes * (p % SIDES) + 1), values)
    values = jnp.where(sub == 0, values, 0).astype(F32)
    mine = (lane >= me * capacity) & (lane < (me + 1) * capacity)
    for m in range(members):
        shift = lax.rem((me - m) * capacity + LANES * members, LANES)
        msg_ref[m, NF * ROWS :, :] = jnp.where(mine, pltpu.roll(values, shift, 1), 0.0)
    width = 2 * PS
    copies[2].wait()
    copies[3].wait()
    for f in range(NF):
        left = left_ref[f, 0:ROWS, :]
        right = pltpu.roll(right_ref[f, 0:ROWS, :], width, 1)
        for g in range(1, blocks):
            rows = slice(g * ROWS, (g + 1) * ROWS)
            here = lane // width == g
            left = jnp.where(here, pltpu.roll(left_ref[f, rows, :], width * g, 1), left)
            edge = right_ref[f, rows, :]
            shift = (width * (g + 1)) % LANES
            right = jnp.where(here, pltpu.roll(edge, shift, 1) if shift else edge, right)
        for m in range(members):
            below = jnp.full((ROWS, LANES), m, I32) < me
            msg_ref[m, f * ROWS : (f + 1) * ROWS, :] = jnp.where(below, left, right)
    outs = [pltpu.make_async_copy(msg_ref, msg_hbm, out_sem.at[0])]
    outs[0].start()
    patch_y = y_cells // PS
    patch_x = chunks * LANES // PS // PS
    x_cell = (lane % PS) * (LANES // PS) + lane // PS
    for s in range(SIDES):
        for ky in range(patch_y):
            code = jnp.zeros((ROWS, LANES), I32)
            for kx in range(patch_x):
                slot = slots[(ky * patch_x + kx) * SIDES + s]
                code = jnp.where(x_cell // PS == kx, slot, code)
            code_ref[s * patch_y + ky] = code + (x_cell // RATIO) % CF * (members * capacity)
    copies[4].wait()
    copies[5].wait()
    for f in range(NF):
        for j in range(chunks // 4):
            low = high = None
            for k in range(4):
                c = slice((4 * j + k) * LANES, (4 * j + k + 1) * LANES)
                first = low_ref[f, :, c]
                last = high_ref[f, :, c]
                first = pltpu.roll(first, 2 * k, 0) if k else first
                last = pltpu.roll(last, 2 * k + 2, 0) if k < 3 else last
                low = first if k == 0 else jnp.where(sub // 2 == k, first, low)
                high = last if k == 0 else jnp.where(sub // 2 == k, last, high)
            lo_ref[f, j * ROWS : (j + 1) * ROWS, :] = low
            hi_ref[f, j * ROWS : (j + 1) * ROWS, :] = high
    outs.append(pltpu.make_async_copy(lo_ref, lo_hbm, out_sem.at[1]))
    outs.append(pltpu.make_async_copy(hi_ref, hi_hbm, out_sem.at[2]))
    outs[1].start()
    outs[2].start()
    for copy in outs:
        copy.wait()


def build_kernel(
    fine_ref, coarse_hbm, wz_hbm, tab_ref, wn_ref, wz_ref, cs_ref, ct_ref, coarse_sem, wz_sem
):
    chunks = fine_ref.shape[2] // LANES
    blocks = fine_ref.shape[1] // ROWS
    coarse_copies = [
        pltpu.make_async_copy(coarse_hbm.at[f], cs_ref.at[f], coarse_sem.at[f]) for f in range(NF)
    ]
    for copy in coarse_copies:
        copy.start()
    lane = iota((ROWS, LANES), 1)

    def turn(block, carry):
        rows = pl.ds(pl.multiple_of(block * ROWS, ROWS), ROWS)
        for c in range(chunks):
            prim = to_primitive(
                [fine_ref[f, rows, c * LANES : (c + 1) * LANES] for f in range(NF)]
            )
            for f in range(NF):
                wn_ref[f, c] = prim[f]
        for f in range(NF):
            tiles = swap_groups([wn_ref[f, c] for c in range(chunks)], lane)
            for z in range(PS):
                wz_ref[f, z, rows, :] = tiles[z]
        return carry

    lax.fori_loop(0, blocks, turn, 0)
    wz_copy = pltpu.make_async_copy(wz_ref, wz_hbm, wz_sem.at[0])
    wz_copy.start()
    sub = iota((ROWS, LANES), 0)
    boxes = coarse_hbm.shape[1]
    for f in range(NF):
        coarse_copies[f].wait()
        for j in range(CB * CB * CB // LANES):
            at = slice(j * LANES, (j + 1) * LANES)
            ct_ref[f, at, :] = cs_ref[f, :, at].T
    for s in range(SIDES):
        middle = CB - 3 if s == 0 else 2

        def cells(z, y):
            at = (z * CB + y) * CB
            return to_primitive([ct_ref[f, at : at + CB, :] for f in range(NF)])

        centre = {y: cells(middle, y) for y in range(1, CB - 1)}
        found = {}
        for cy in range(CF):
            y = cy + 2
            below, above = cells(middle - 1, y), cells(middle + 1, y)
            for f in range(NF):
                c = centre[y][f]
                found[f, 0, cy] = c
                found[f, 1, cy] = minmod(c - below[f], above[f] - c)
                found[f, 2, cy] = minmod(c - centre[y - 1][f], centre[y + 1][f] - c)
                found[f, 3, cy] = minmod(c - pltpu.roll(c, 1, 0), pltpu.roll(c, ROWS - 1, 0) - c)
        for f in range(NF):
            for q in range(QUANT):
                at = (f * QUANT + q) * CF * CF
                for i in range(2):
                    tab_ref[at + i * ROWS : at + (i + 1) * ROWS, s * boxes : (s + 1) * boxes] = (
                        jnp.where(
                            sub < CF,
                            pltpu.roll(found[f, q, 2 * i], ROWS - 2, 0),
                            pltpu.roll(found[f, q, 2 * i + 1], 2, 0),
                        )
                    )
    wz_copy.wait()


def serve_kernel(msg_ref, tab_ref, out_hbm, hot_ref, out_ref, sem_ref):
    members = msg_ref.shape[0]
    slot_count = out_ref.shape[0]
    row = msg_ref[0, NF * ROWS :, :]
    for m in range(1, members):
        row = row + msg_ref[m, NF * ROWS :, :]
    shape = (slot_count, LANES)
    wide = jnp.broadcast_to(row[0:1, :], shape)
    column = jnp.sum(jnp.where(iota(shape, 0) == iota(shape, 1), wide, 0.0), axis=1, keepdims=True)
    target = column.astype(I32) - 1
    hot = jnp.where(iota(hot_ref.shape, 1) == target, 1.0, 0.0).astype(BF16)
    hot_ref[...] = hot
    total = None
    for part in split3(tab_ref[...]):
        got = lax.dot_general(
            hot, part, (((1,), (1,)), ((), ())), preferred_element_type=F32
        )
        total = got if total is None else total + got
    out_ref[:, 0:TABLE_ROWS] = total
    out_ref[:, TABLE_ROWS:] = jnp.zeros((slot_count, TABLE_PAD - TABLE_ROWS), F32)
    copy = pltpu.make_async_copy(out_ref, out_hbm, sem_ref.at[0])
    copy.start()
    copy.wait()


def sweep_line(tiles, normal, back, forward, emit, finish=None):
    fields = range(NF)
    last = len(tiles) - 1
    moved = [[back(None, t[f]) for f in fields] for t in tiles]
    diff = [
        [t[f] - back(moved[max(i - 1, 0)][f], moved[i][f]) for f in fields]
        for i, t in enumerate(tiles)
    ]
    diff_moved = [[forward(None, d[f]) for f in fields] for d in diff]
    low_moved = None
    flux = flux_moved = None
    for i, t in enumerate(tiles):
        half = [
            0.5 * minmod(diff[i][f], forward(diff_moved[i][f], diff_moved[min(i + 1, last)][f]))
            for f in fields
        ]
        if i == last and finish is not None:
            finish(low_moved, [t[f] - half[f] for f in fields], flux, flux_moved)
            return
        low_next = [back(None, t[f] + half[f]) for f in fields]
        if i > 0:
            left = [back(low_moved[f], low_next[f]) for f in fields]
            new = hll(left, [t[f] - half[f] for f in fields], normal)
            new_moved = [forward(None, new[f]) for f in fields]
            if i > 1:
                emit(i - 2, [forward(flux_moved[f], new_moved[f]) - flux[f] for f in fields])
            flux, flux_moved = new, new_moved
        low_moved = low_next


def groups_of(start, stop):
    return [(at, min(ROWS, stop - at)) for at in range(start, stop, ROWS)]


def y_columns(start, count, skip, blocks, lo_ref, hi_ref, load, add):
    sub = iota((ROWS, LANES), 0)

    def y_back(before, here):
        if before is None:
            return pltpu.roll(here, 1, 0)
        return jnp.where(sub < 1, before, here)

    def y_forward(here, after):
        if here is None:
            return pltpu.roll(after, ROWS - 1, 0)
        return jnp.where(sub >= ROWS - 1, after, here)

    ends = []
    for k in range(count):
        c = start + k
        at = slice((c - skip) // 4 * ROWS, ((c - skip) // 4 + 1) * ROWS)
        if k % 4 == 0:
            low = to_primitive([lo_ref[f, at, :] for f in range(NF)])
            high = to_primitive([hi_ref[f, at, :] for f in range(NF)])
        turn_low, turn_high = (6 - 2 * (k % 4)) % ROWS, (ROWS - 2 * (k % 4)) % ROWS
        below = [pltpu.roll(t, turn_low, 0) if turn_low else t for t in low]
        above = [pltpu.roll(t, turn_high, 0) if turn_high else t for t in high]
        tiles = [load(c, b) for b in range(blocks)]

        def emit(b, change):
            for f in range(NF):
                add(f, c, b, change[f])

        sweep_line(
            [below] + tiles + [above], 1, y_back, y_forward, emit, lambda *end: ends.append(end)
        )
    packed = []
    for which in range(2):
        state = []
        for f in range(NF):
            tile = ends[0][which][f]
            for k in range(1, count):
                tile = jnp.where(sub == k, pltpu.roll(ends[k][which][f], k, 0), tile)
            state.append(tile)
        packed.append(state)
    top = hll(packed[0], packed[1], 1)
    for k in range(count):
        c = start + k
        flux, flux_moved = ends[k][2], ends[k][3]
        for f in range(NF):
            moved = pltpu.roll(top[f], ROWS - 1 - k, 0) if k < ROWS - 1 else top[f]
            change = y_forward(flux_moved[f], moved) - flux[f]
            add(f, c, blocks - 1, change)


def plane_kernel(
    members, msg_ref, lo_hbm, hi_hbm, fine_ref, after_ref, wz_hbm,
    out_ref, near_ref, ends_ref, wn_ref, lo_ref, hi_ref, sem_ref,
):
    near_copies = [
        pltpu.make_async_copy(
            wz_hbm.at[:, start : start + NEAR],
            near_ref.at[:, i * NEAR : (i + 1) * NEAR],
            sem_ref.at[i],
        )
        for i, start in enumerate((0, PS - NEAR))
    ]
    end_copies = [
        pltpu.make_async_copy(lo_hbm, lo_ref, sem_ref.at[2]),
        pltpu.make_async_copy(hi_hbm, hi_ref, sem_ref.at[3]),
    ]
    for copy in near_copies + end_copies:
        copy.start()
    me = lax.axis_index("dev")
    chunks = fine_ref.shape[2] // LANES
    blocks = fine_ref.shape[1] // ROWS
    lane = iota((ROWS, LANES), 1)
    width = 2 * PS
    place = jnp.full((ROWS, LANES), me, I32)

    def x_back(before, here):
        if before is None:
            return pltpu.roll(here, PS, 1)
        return jnp.where(lane < PS, before, here)

    def x_forward(here, after):
        if here is None:
            return pltpu.roll(after, LANES - PS, 1)
        return jnp.where(lane >= LANES - PS, after, here)

    def x_block(block, carry):
        rows = pl.ds(pl.multiple_of(block * ROWS, ROWS), ROWS)
        left = jnp.maximum(me - 1, 0)
        right = jnp.minimum(me + 1, members - 1)
        shift_low = lax.rem(2 * LANES - width - width * block, LANES)
        shift_high = lax.rem(LANES - width * block, LANES)
        low = to_primitive(
            [pltpu.roll(msg_ref[left, f * ROWS : (f + 1) * ROWS, :], shift_low, 1) for f in range(NF)]
        )
        high = to_primitive(
            [pltpu.roll(msg_ref[right, f * ROWS : (f + 1) * ROWS, :], shift_high, 1) for f in range(NF)]
        )
        tiles = []
        for c in range(chunks):
            prim = to_primitive(
                [fine_ref[f, rows, c * LANES : (c + 1) * LANES] for f in range(NF)]
            )
            for f in range(NF):
                wn_ref[f, c, rows, :] = prim[f]
            tiles.append(prim)
        for f in range(NF):
            w = tiles[0][f]
            same = jnp.where(
                lane < LANES - PS, pltpu.roll(w, LANES - width, 1), pltpu.roll(w, LANES - PS, 1)
            )
            low[f] = jnp.where(place == 0, same, low[f])
            w = tiles[-1][f]
            same = jnp.where(lane < PS, pltpu.roll(w, PS, 1), pltpu.roll(w, width, 1))
            high[f] = jnp.where(place == members - 1, same, high[f])

        def emit(c, change):
            at = slice(c * LANES, (c + 1) * LANES)
            for f in range(NF):
                out_ref[f, c, rows, :] = fine_ref[f, rows, at] - DT_DX * change[f]

        sweep_line([low] + tiles + [high], 0, x_back, x_forward, emit)
        return carry

    lax.fori_loop(0, blocks, x_block, 0)

    def load(c, b):
        return [wn_ref[f, c, b * ROWS : (b + 1) * ROWS, :] for f in range(NF)]

    def add(f, c, b, change):
        at = slice(b * ROWS, (b + 1) * ROWS)
        out_ref[f, c, at, :] = out_ref[f, c, at, :] - DT_DX * change

    for copy in end_copies:
        copy.wait()
    ends_ref[0] = lo_ref[:, 2 * Y_EARLY :, :]
    ends_ref[1] = hi_ref[:, 2 * Y_EARLY :, :]
    for start, count in groups_of(0, Y_EARLY):
        y_columns(start, count, 0, blocks, lo_ref, hi_ref, load, add)
    for copy in near_copies:
        copy.wait()


def face_kernel(
    slot_count, got_ref, code_ref, near_ref, after_ref, term_hbm, edge_hbm,
    edge_ref, he_ref, rt_ref, lf_ref, g_ref, v_ref, term_ref, sem_ref,
):
    lane = iota((ROWS, LANES), 1)
    sub = iota((ROWS, LANES), 0)
    rows_all = NF * QUANT * CF
    y_cells = near_ref.shape[2]
    blocks = y_cells // ROWS
    patch_y = y_cells // PS
    number = iota((CF * slot_count, LANES), 0)
    for i in range(code_ref.shape[0]):
        hot = jnp.where(number == code_ref[i, 0:1, :], 1.0, 0.0)
        he_ref[:, i * LANES : (i + 1) * LANES] = hot.astype(BF16)
    rt_ref[...] = got_ref[...].T
    for cx in range(CF):
        lf_ref[:, cx * slot_count : (cx + 1) * slot_count] = rt_ref[
            pl.ds(cx, rows_all, stride=CF), :
        ]
    parts = jnp.concatenate(split3(lf_ref[...]), axis=0)
    product = jnp.dot(parts, he_ref[...], preferred_element_type=F32)
    g_ref[...] = (
        product[0:rows_all] + product[rows_all : 2 * rows_all] + product[2 * rows_all :]
    )

    def pick(options, index):
        value = jnp.full((ROWS, LANES), options[0], F32)
        for i in range(1, RATIO):
            value = jnp.where(index == i, options[i], value)
        return value

    off_y = pick(OFFSETS, sub % RATIO)
    off_x = pick(OFFSETS, (lane // PS) % RATIO)
    for block in range(blocks):
        ky, half = block // (blocks // patch_y), block % (blocks // patch_y)
        rows = slice(block * ROWS, (block + 1) * ROWS)
        for s in range(SIDES):
            at = (s * patch_y + ky) * LANES
            ghosts = [[], []]
            for f in range(NF):
                terms = []
                for q in range(QUANT):
                    r = (f * QUANT + q) * CF + 2 * half
                    terms.append(
                        jnp.where(
                            sub < RATIO,
                            jnp.broadcast_to(g_ref[r : r + 1, at : at + LANES], (ROWS, LANES)),
                            jnp.broadcast_to(g_ref[r + 1 : r + 2, at : at + LANES], (ROWS, LANES)),
                        )
                    )
                for i in range(2):
                    off_z = OFFSETS[i + (RATIO - 2 if s == 0 else 0)]
                    ghosts[i].append(
                        ((terms[0] + terms[1] * off_z) + terms[2] * off_y) + terms[3] * off_x
                    )

            inner = [
                [near_ref[f, NEAR * s + i, rows, :] for f in range(NF)] for i in range(NEAR)
            ]
            line = ghosts + inner if s == 0 else inner + ghosts
            diff = [[line[i + 1][f] - line[i][f] for f in range(NF)] for i in range(4)]
            half_slope = [
                [0.5 * minmod(diff[i][f], diff[i + 1][f]) for f in range(NF)] for i in range(3)
            ]
            low = [[line[i + 1][f] + half_slope[i][f] for f in range(NF)] for i in range(2)]
            up = [[line[i + 2][f] - half_slope[i + 1][f] for f in range(NF)] for i in range(2)]
            flux = hll(low[s], up[s], 2)
            state = low[1] if s == 0 else up[0]
            for f in range(NF):
                edge_ref[f, 2 * s, rows, :] = flux[f]
                edge_ref[f, 2 * s + 1, rows, :] = state[f]

    edge_copy = pltpu.make_async_copy(edge_ref, edge_hbm, sem_ref.at[1])
    edge_copy.start()
    v_ref[NF * CF :, :] = jnp.zeros((TERM_ROWS - NF * CF, v_ref.shape[1]), F32)
    for s in range(SIDES):
        for f in range(NF):
            total = None
            for i in range(RATIO):
                got = edge_ref[f, 2 * s, pl.ds(i, y_cells // RATIO, stride=RATIO), :]
                total = got if total is None else total + got
            total = total * (1.0 / RATIO)
            for ky in range(patch_y):
                at = (s * patch_y + ky) * LANES
                v_ref[f * CF : (f + 1) * CF, at : at + LANES] = total[ky * CF : (ky + 1) * CF]
    parts = jnp.concatenate(split3(v_ref[...]), axis=0)
    product = lax.dot_general(
        parts, he_ref[...], (((1,), (1,)), ((), ())), preferred_element_type=F32
    )
    summed = (
        product[0:TERM_ROWS] + product[TERM_ROWS : 2 * TERM_ROWS] + product[2 * TERM_ROWS :]
    )
    turned = summed.T
    for cx in range(CF):
        term_ref[:, cx * TERM_ROWS : (cx + 1) * TERM_ROWS] = turned[
            cx * slot_count : (cx + 1) * slot_count, :
        ]
    copy = pltpu.make_async_copy(term_ref, term_hbm, sem_ref.at[0])
    copy.start()
    edge_copy.wait()
    copy.wait()


def final_kernel(
    fine_ref, plane_ref, edge_hbm, ends_ref, wz_hbm, out_hbm,
    edge_ref, wz_ref, zc_ref, extra_ref, out_ref, wz_sem, out_sem,
):
    lane = iota((ROWS, LANES), 1)
    chunks = plane_ref.shape[1]
    blocks = plane_ref.shape[2] // ROWS

    def wz_copy(block):
        rows = pl.ds(pl.multiple_of(block * ROWS, ROWS), ROWS)
        return pltpu.make_async_copy(
            wz_hbm.at[:, :, rows, :], wz_ref.at[:, :, rows, :], wz_sem.at[block]
        )

    def out_copy(block):
        rows = pl.ds(pl.multiple_of(block * ROWS, ROWS), ROWS)
        return pltpu.make_async_copy(
            out_ref.at[:, rows, :], out_hbm.at[:, rows, :], out_sem.at[block]
        )

    edge_copy = pltpu.make_async_copy(edge_hbm, edge_ref, wz_sem.at[blocks])
    edge_copy.start()
    for block in range(blocks):
        wz_copy(block).start()
    first = Y_EARLY

    def load(c, b):
        at = slice(b * ROWS, (b + 1) * ROWS)
        return to_primitive([fine_ref[f, at, c * LANES : (c + 1) * LANES] for f in range(NF)])

    def add(f, c, b, change):
        at = slice(b * ROWS, (b + 1) * ROWS)
        extra_ref[f, c - first, at, :] = plane_ref[f, c, at, :] - DT_DX * change

    for start, count in groups_of(first, chunks):
        y_columns(start, count, first, blocks, ends_ref.at[0], ends_ref.at[1], load, add)

    edge_copy.wait()

    def step(block, carry):
        rows = pl.ds(pl.multiple_of(block * ROWS, ROWS), ROWS)
        wz_copy(block).wait()

        def load(z):
            return [wz_ref[f, z, rows, :] for f in range(NF)]

        def edge(i):
            return [edge_ref[f, i, rows, :] for f in range(NF)]

        w_here = load(1)
        w_before = load(0)
        diff = [w_here[f] - w_before[f] for f in range(NF)]
        flux, low = edge(0), edge(1)
        for z in range(1, PS):
            if z < PS - 1:
                w_next = load(z + 1)
                diff_next = [w_next[f] - w_here[f] for f in range(NF)]
                half = [0.5 * minmod(diff[f], diff_next[f]) for f in range(NF)]
                up = [w_here[f] - half[f] for f in range(NF)]
            else:
                up = edge(3)
            new = hll(low, up, 2)
            for f in range(NF):
                zc_ref[f, z - 1] = new[f] - flux[f]
            flux = new
            if z < PS - 1:
                low = [w_here[f] + half[f] for f in range(NF)]
                w_here, diff = w_next, diff_next
        new = edge(2)
        for f in range(NF):
            zc_ref[f, PS - 1] = new[f] - flux[f]
        for f in range(NF):
            tiles = [zc_ref[f, z] for z in range(PS)]
            tiles = swap_groups(tiles, lane)
            for c in range(chunks):
                at = slice(c * LANES, (c + 1) * LANES)
                if c < first:
                    partial = plane_ref[f, c, rows, :]
                else:
                    partial = extra_ref[f, c - first, rows, :]
                out_ref[f, rows, at] = partial - DT_DX * tiles[c]
        out_copy(block).start()
        return carry

    lax.fori_loop(0, blocks, step, 0)

    for block in range(blocks):
        out_copy(block).wait()


def register_kernel(got_ref, hot_ref, out_ref, z_ref):
    boxes = out_ref.shape[2]
    turned = got_ref[...].T
    parts = jnp.concatenate(split3(turned), axis=0)
    product = jnp.dot(parts, hot_ref[...], preferred_element_type=F32)
    z_ref[...] = product[0:LANES] + product[LANES : 2 * LANES] + product[2 * LANES :]
    for f in range(NF):
        for cx in range(CF):
            at = cx * TERM_ROWS + f * CF
            for s in range(SIDES):
                out_ref[f, pl.ds(s * CF * CF + cx, CF, stride=CF), :] = z_ref[
                    at : at + CF, s * boxes : (s + 1) * boxes
                ]


VM = pl.BlockSpec(memory_space=pltpu.VMEM)
HB = pl.BlockSpec(memory_space=pltpu.HBM)


def call(body, ins, outs, out_specs, scratch=(), cost=0, limit=8 << 10):
    kernel = pl.pallas_call(
        body,
        in_specs=list(ins),
        out_specs=list(out_specs),
        out_shape=[
            pltpu.HBM(o.shape, o.dtype) if spec is HB else o for o, spec in zip(outs, out_specs)
        ],
        scratch_shapes=list(scratch),
        compiler_params=pltpu.CompilerParams(vmem_limit_bytes=limit << 10),
        cost_estimate=pl.CostEstimate(flops=cost, bytes_accessed=cost, transcendentals=0),
    )

    def run(*args):
        return kernel(
            *[
                pltpu.with_memory_space_constraint(a, pltpu.HBM) if spec is HB else a
                for a, spec in zip(args, ins)
            ]
        )

    return run


def shaped(*shape, dtype=F32):
    return jax.ShapeDtypeStruct(shape, dtype)


def local(members, groups, fine_state, coarse_boxes, piece_owner, piece_box):
    y_cells = fine_state.shape[1]
    x_cells = fine_state.shape[2] // PS
    boxes = coarse_boxes.shape[0]
    pieces = piece_box.shape[0]
    capacity = max(4, 2 * pieces // members)
    slots = members * capacity
    chunks = x_cells * PS // LANES
    blocks = y_cells // ROWS
    patch_y = y_cells // PS
    assert chunks == PS and boxes == LANES and slots <= LANES and PS == QS
    assert y_cells == 4 * ROWS and pieces == SIDES * patch_y * (x_cells // PS)
    edge_rows = 2 * chunks
    rows_all = NF * QUANT * CF
    wide = SIDES * patch_y * LANES
    count = pltpu.SMEM((members,), I32)
    piece_list = pltpu.SMEM((pieces,), I32)
    dma = pltpu.SemaphoreType.DMA
    fine_shape = fine_state.shape
    vmem = lambda *shape: pltpu.VMEM(shape, F32)
    owners = piece_owner.reshape(pieces)

    msg_shape = (members, (NF + 1) * ROWS, LANES)
    edge_shape = (NF, edge_rows, LANES)
    msg, low_edge, high_edge, code = call(
        functools.partial(prep_kernel, members, capacity, boxes),
        (HB, HB, HB),
        [
            shaped(*msg_shape), shaped(*edge_shape), shaped(*edge_shape),
            shaped(SIDES * patch_y, ROWS, LANES, dtype=I32),
        ],
        (HB, HB, HB, VM),
        [
            piece_list, piece_list, count,
            vmem(NF, ROWS, fine_shape[2]), vmem(NF, ROWS, fine_shape[2]),
            vmem(NF, y_cells, LANES), vmem(NF, y_cells, LANES),
            vmem(*msg_shape), vmem(*edge_shape), vmem(*edge_shape),
            dma((6,)), dma((3,)),
        ],
        cost=1 << 18,
    )(owners, piece_box, fine_state)
    got = lax.all_to_all(msg, "dev", split_axis=0, concat_axis=0, tiled=True)
    up = [(g, (g + 1) % groups) for g in range(groups)]
    down = [(b, a) for a, b in up]
    y_low = lax.ppermute(high_edge, "group", up)
    y_high = lax.ppermute(low_edge, "group", down)

    turned_shape = (NF, PS, y_cells, LANES)
    build = call(
        build_kernel,
        (VM, HB),
        [
            shaped(*turned_shape),
            shaped(TABLE_ROWS, SIDES * boxes),
        ],
        (HB, VM),
        [
            vmem(NF, chunks, ROWS, LANES),
            vmem(*turned_shape),
            vmem(NF, boxes, CB * CB * CB),
            vmem(NF, CB * CB * CB, boxes),
            dma((NF,)),
            dma((1,)),
        ],
        cost=1 << 23,
    )
    wz, table = build(fine_state, coarse_boxes.transpose(1, 0, 2))
    payload, hot_box = call(
        serve_kernel,
        (VM, VM),
        [shaped(slots, TABLE_PAD), shaped(slots, SIDES * boxes, dtype=BF16)],
        (HB, VM),
        [vmem(slots, TABLE_PAD), dma((1,))],
        cost=1 << 18,
    )(got, table)
    back = lax.all_to_all(payload, "dev", split_axis=0, concat_axis=0, tiled=True)

    plane, near, ends = call(
        functools.partial(plane_kernel, members),
        (VM, HB, HB, VM, VM, HB),
        [
            shaped(NF, chunks, y_cells, LANES),
            shaped(NF, 2 * NEAR, y_cells, LANES),
            shaped(2, NF, edge_rows - 2 * Y_EARLY, LANES),
        ],
        (VM, VM, VM),
        [
            vmem(NF, chunks, y_cells, LANES),
            vmem(*edge_shape),
            vmem(*edge_shape),
            dma((4,)),
        ],
        cost=1 << 24,
    )(got, y_low, y_high, fine_state, hot_box, wz)

    terms, edge = call(
        functools.partial(face_kernel, slots),
        (VM, VM, VM, VM),
        [shaped(slots, LANES), shaped(NF, 4, y_cells, LANES)],
        (HB, HB),
        [
            vmem(NF, 4, y_cells, LANES),
            pltpu.VMEM((CF * slots, wide), BF16),
            vmem(TABLE_PAD, slots),
            vmem(rows_all, CF * slots),
            vmem(rows_all, wide),
            vmem(TERM_ROWS, wide),
            vmem(slots, LANES),
            dma((2,)),
        ],
        cost=1 << 20,
    )(back, code, near, plane)
    incoming = lax.all_to_all(terms, "dev", split_axis=0, concat_axis=0, tiled=True)

    (fine_next,) = call(
        final_kernel,
        (VM, VM, HB, VM, HB),
        [shaped(*fine_shape)],
        (HB,),
        [
            vmem(NF, 4, y_cells, LANES),
            vmem(*turned_shape),
            vmem(NF, PS, ROWS, LANES),
            vmem(NF, chunks - Y_EARLY, y_cells, LANES),
            vmem(*fine_shape),
            dma((blocks + 1,)),
            dma((blocks,)),
        ],
        cost=1 << 24,
    )(fine_state, plane, edge, ends, wz)
    (flux_register,) = call(
        register_kernel,
        (VM, VM),
        [shaped(NF, SIDES * CF * CF, boxes)],
        (VM,),
        [vmem(LANES, SIDES * boxes)],
        cost=1 << 18,
    )(incoming, hot_box)
    return (fine_next, flux_register)


def solution(mesh):
    in_specs = (
        P(None, "group", "dev"),
        P(("group", "dev"), None, None),
        P(("group", "dev"), None),
        P(("group", "dev")),
    )
    out_specs = (P(None, "group", "dev"), P(None, None, ("group", "dev")))
    body = functools.partial(local, mesh.shape["dev"], mesh.shape["group"])
    return jax.shard_map(body, mesh=mesh, in_specs=in_specs, out_specs=out_specs, check_vma=False)
```

```python
import functools

import jax
import jax.numpy as jnp
from jax import lax
from jax.experimental import pallas as pl
from jax.experimental.pallas import tpu as pltpu
from jax.sharding import PartitionSpec as P


PS = 16
RATIO = 4
QS = 16
CF = 4
CB = 8
NF = 5
LANES = 128
ROWS = 8
SIDES = 2
QUANT = 4

GAMMA = 1.4
DT_DX = 0.08
OFFSETS = [(i + 0.5) / RATIO - 0.5 for i in range(RATIO)]
F32, BF16, I32 = jnp.float32, jnp.bfloat16, jnp.int32
TABLE_ROWS = NF * QUANT * CF * CF
TABLE_PAD = 384
TERM_ROWS = 32
Y_EARLY = 8
NEAR = 2


def iota(shape, dim):
    return lax.broadcasted_iota(I32, shape, dim)


def minmod(a, b):
    return jnp.maximum(jnp.minimum(a, b), 0.0) + jnp.minimum(jnp.maximum(a, b), 0.0)


def to_primitive(cons):
    inverse = 1.0 / cons[0]
    velocity = [cons[1 + i] * inverse for i in range(3)]
    kinetic = cons[1] * velocity[0] + cons[2] * velocity[1] + cons[3] * velocity[2]
    return [cons[0]] + velocity + [(GAMMA - 1.0) * (cons[4] - 0.5 * kinetic)]


def hll(low, up, normal):
    others = [1 + i for i in range(3) if i != normal]
    u_low, u_up = low[1 + normal], up[1 + normal]
    p_low, p_up = low[4], up[4]
    g_low, g_up = GAMMA * p_low, GAMMA * p_up
    c_low = g_low * lax.rsqrt(g_low * low[0])
    c_up = g_up * lax.rsqrt(g_up * up[0])
    slow = jnp.minimum(jnp.minimum(u_low - c_low, u_up - c_up), 0.0)
    fast = jnp.maximum(jnp.maximum(u_low + c_low, u_up + c_up), 0.0)
    inverse = 1.0 / (fast - slow)
    f = fast * inverse
    s = slow * inverse
    a = f * (u_low - slow)
    b = s * (u_up - fast)
    m_low = a * low[0]
    m_up = b * up[0]
    k_low = 0.5 * (low[1] * low[1] + low[2] * low[2] + low[3] * low[3])
    k_up = 0.5 * (up[1] * up[1] + up[2] * up[2] + up[3] * up[3])
    rest = 1.0 / (GAMMA - 1.0)
    flux = [m_low - m_up, None, None, None, None]
    for i in others:
        flux[i] = m_low * low[i] - m_up * up[i]
    flux[1 + normal] = (m_low * u_low + f * p_low) - (m_up * u_up + s * p_up)
    flux[4] = (m_low * k_low + p_low * (rest * a + f * u_low)) - (
        m_up * k_up + p_up * (rest * b + s * u_up)
    )
    return flux


def split3(x):
    high = x.astype(BF16)
    left = x - high.astype(F32)
    middle = left.astype(BF16)
    low = (left - middle.astype(F32)).astype(BF16)
    return [high, middle, low]


def swap_groups(tiles, lane):
    count = len(tiles)
    tiles = [pltpu.roll(t, c, 1) if c else t for c, t in enumerate(tiles)]
    step = 1
    while step < count:
        odd = lane // step % 2 == 1
        tiles = [jnp.where(odd, tiles[(i + step) % count], tiles[i]) for i in range(count)]
        step *= 2
    return [
        pltpu.roll(tiles[count - z], LANES - z, 1) if z else tiles[0] for z in range(count)
    ]


def count_slots(owner_ref, count_ref, members, capacity, pieces):
    for m in range(members):
        count_ref[m] = 0
    slots = []
    for p in range(pieces):
        owner = owner_ref[p]
        rank = count_ref[owner]
        count_ref[owner] = rank + 1
        slots.append(owner * capacity + rank)
    return slots


def prep_kernel(
    members, capacity, boxes, owner_hbm, box_hbm, fine_hbm, msg_hbm, lo_hbm, hi_hbm, code_ref,
    owner_ref, box_ref, count_ref, low_ref, high_ref, left_ref, right_ref,
    msg_ref, lo_ref, hi_ref, sem_ref, out_sem,
):
    me = lax.axis_index("dev")
    pieces = box_hbm.shape[0]
    y_cells = fine_hbm.shape[1]
    chunks = fine_hbm.shape[2] // LANES
    blocks = y_cells // ROWS
    ends = [
        (owner_hbm, owner_ref),
        (box_hbm, box_ref),
        (fine_hbm.at[:, :, 0:LANES], left_ref),
        (fine_hbm.at[:, :, (chunks - 1) * LANES : chunks * LANES], right_ref),
        (fine_hbm.at[:, 0:2, :], low_ref.at[:, 0:2, :]),
        (fine_hbm.at[:, y_cells - 2 : y_cells, :], high_ref.at[:, ROWS - 2 : ROWS, :]),
    ]
    copies = [pltpu.make_async_copy(a, b, sem_ref.at[i]) for i, (a, b) in enumerate(ends)]
    for copy in copies:
        copy.start()
    lane = iota((ROWS, LANES), 1)
    sub = iota((ROWS, LANES), 0)
    copies[0].wait()
    copies[1].wait()
    slots = count_slots(owner_ref, count_ref, members, capacity, pieces)
    values = jnp.zeros((ROWS, LANES), I32)
    for p in range(pieces):
        values = jnp.where(lane == slots[p], box_ref[p] + (boxes * (p % SIDES) + 1), values)
    values = jnp.where(sub == 0, values, 0).astype(F32)
    mine = (lane >= me * capacity) & (lane < (me + 1) * capacity)
    for m in range(members):
        shift = lax.rem((me - m) * capacity + LANES * members, LANES)
        msg_ref[m, NF * ROWS :, :] = jnp.where(mine, pltpu.roll(values, shift, 1), 0.0)
    width = 2 * PS
    copies[2].wait()
    copies[3].wait()
    for f in range(NF):
        left = left_ref[f, 0:ROWS, :]
        right = pltpu.roll(right_ref[f, 0:ROWS, :], width, 1)
        for g in range(1, blocks):
            rows = slice(g * ROWS, (g + 1) * ROWS)
            here = lane // width == g
            left = jnp.where(here, pltpu.roll(left_ref[f, rows, :], width * g, 1), left)
            edge = right_ref[f, rows, :]
            shift = (width * (g + 1)) % LANES
            right = jnp.where(here, pltpu.roll(edge, shift, 1) if shift else edge, right)
        for m in range(members):
            below = jnp.full((ROWS, LANES), m, I32) < me
            msg_ref[m, f * ROWS : (f + 1) * ROWS, :] = jnp.where(below, left, right)
    outs = [pltpu.make_async_copy(msg_ref, msg_hbm, out_sem.at[0])]
    outs[0].start()
    patch_y = y_cells // PS
    patch_x = chunks * LANES // PS // PS
    x_cell = (lane % PS) * (LANES // PS) + lane // PS
    for s in range(SIDES):
        for ky in range(patch_y):
            code = jnp.zeros((ROWS, LANES), I32)
            for kx in range(patch_x):
                slot = slots[(ky * patch_x + kx) * SIDES + s]
                code = jnp.where(x_cell // PS == kx, slot, code)
            code_ref[s * patch_y + ky] = code + (x_cell // RATIO) % CF * (members * capacity)
    copies[4].wait()
    copies[5].wait()
    for f in range(NF):
        for j in range(chunks // 4):
            low = high = None
            for k in range(4):
                c = slice((4 * j + k) * LANES, (4 * j + k + 1) * LANES)
                first = low_ref[f, :, c]
                last = high_ref[f, :, c]
                first = pltpu.roll(first, 2 * k, 0) if k else first
                last = pltpu.roll(last, 2 * k + 2, 0) if k < 3 else last
                low = first if k == 0 else jnp.where(sub // 2 == k, first, low)
                high = last if k == 0 else jnp.where(sub // 2 == k, last, high)
            lo_ref[f, j * ROWS : (j + 1) * ROWS, :] = low
            hi_ref[f, j * ROWS : (j + 1) * ROWS, :] = high
    outs.append(pltpu.make_async_copy(lo_ref, lo_hbm, out_sem.at[1]))
    outs.append(pltpu.make_async_copy(hi_ref, hi_hbm, out_sem.at[2]))
    outs[1].start()
    outs[2].start()
    for copy in outs:
        copy.wait()


def build_kernel(
    fine_ref, coarse_hbm, wz_hbm, tab_ref, wn_ref, wz_ref, cs_ref, ct_ref, coarse_sem, wz_sem
):
    chunks = fine_ref.shape[2] // LANES
    blocks = fine_ref.shape[1] // ROWS
    coarse_copies = [
        pltpu.make_async_copy(coarse_hbm.at[f], cs_ref.at[f], coarse_sem.at[f]) for f in range(NF)
    ]
    for copy in coarse_copies:
        copy.start()
    lane = iota((ROWS, LANES), 1)

    def turn(block, carry):
        rows = pl.ds(pl.multiple_of(block * ROWS, ROWS), ROWS)
        for c in range(chunks):
            prim = to_primitive(
                [fine_ref[f, rows, c * LANES : (c + 1) * LANES] for f in range(NF)]
            )
            for f in range(NF):
                wn_ref[f, c] = prim[f]
        for f in range(NF):
            tiles = swap_groups([wn_ref[f, c] for c in range(chunks)], lane)
            for z in range(PS):
                wz_ref[f, z, rows, :] = tiles[z]
        return carry

    lax.fori_loop(0, blocks, turn, 0)
    wz_copy = pltpu.make_async_copy(wz_ref, wz_hbm, wz_sem.at[0])
    wz_copy.start()
    sub = iota((ROWS, LANES), 0)
    boxes = coarse_hbm.shape[1]
    for f in range(NF):
        coarse_copies[f].wait()
        for j in range(CB * CB * CB // LANES):
            at = slice(j * LANES, (j + 1) * LANES)
            ct_ref[f, at, :] = cs_ref[f, :, at].T
    for s in range(SIDES):
        middle = CB - 3 if s == 0 else 2

        def cells(z, y):
            at = (z * CB + y) * CB
            return to_primitive([ct_ref[f, at : at + CB, :] for f in range(NF)])

        centre = {y: cells(middle, y) for y in range(1, CB - 1)}
        found = {}
        for cy in range(CF):
            y = cy + 2
            below, above = cells(middle - 1, y), cells(middle + 1, y)
            for f in range(NF):
                c = centre[y][f]
                found[f, 0, cy] = c
                found[f, 1, cy] = minmod(c - below[f], above[f] - c)
                found[f, 2, cy] = minmod(c - centre[y - 1][f], centre[y + 1][f] - c)
                found[f, 3, cy] = minmod(c - pltpu.roll(c, 1, 0), pltpu.roll(c, ROWS - 1, 0) - c)
        for f in range(NF):
            for q in range(QUANT):
                at = (f * QUANT + q) * CF * CF
                for i in range(2):
                    tab_ref[at + i * ROWS : at + (i + 1) * ROWS, s * boxes : (s + 1) * boxes] = (
                        jnp.where(
                            sub < CF,
                            pltpu.roll(found[f, q, 2 * i], ROWS - 2, 0),
                            pltpu.roll(found[f, q, 2 * i + 1], 2, 0),
                        )
                    )
    wz_copy.wait()


def serve_kernel(msg_ref, tab_ref, out_hbm, hot_ref, out_ref, sem_ref):
    members = msg_ref.shape[0]
    slot_count = out_ref.shape[0]
    row = msg_ref[0, NF * ROWS :, :]
    for m in range(1, members):
        row = row + msg_ref[m, NF * ROWS :, :]
    shape = (slot_count, LANES)
    wide = jnp.broadcast_to(row[0:1, :], shape)
    column = jnp.sum(jnp.where(iota(shape, 0) == iota(shape, 1), wide, 0.0), axis=1, keepdims=True)
    target = column.astype(I32) - 1
    hot = jnp.where(iota(hot_ref.shape, 1) == target, 1.0, 0.0).astype(BF16)
    hot_ref[...] = hot
    total = None
    for part in split3(tab_ref[...]):
        got = lax.dot_general(
            hot, part, (((1,), (1,)), ((), ())), preferred_element_type=F32
        )
        total = got if total is None else total + got
    out_ref[:, 0:TABLE_ROWS] = total
    out_ref[:, TABLE_ROWS:] = jnp.zeros((slot_count, TABLE_PAD - TABLE_ROWS), F32)
    copy = pltpu.make_async_copy(out_ref, out_hbm, sem_ref.at[0])
    copy.start()
    copy.wait()


def sweep_line(tiles, normal, back, forward, emit, finish=None):
    fields = range(NF)
    last = len(tiles) - 1
    moved = [[back(None, t[f]) for f in fields] for t in tiles]
    diff = [
        [t[f] - back(moved[max(i - 1, 0)][f], moved[i][f]) for f in fields]
        for i, t in enumerate(tiles)
    ]
    diff_moved = [[forward(None, d[f]) for f in fields] for d in diff]
    low_moved = None
    flux = flux_moved = None
    for i, t in enumerate(tiles):
        half = [
            0.5 * minmod(diff[i][f], forward(diff_moved[i][f], diff_moved[min(i + 1, last)][f]))
            for f in fields
        ]
        if i == last and finish is not None:
            finish(low_moved, [t[f] - half[f] for f in fields], flux, flux_moved)
            return
        low_next = [back(None, t[f] + half[f]) for f in fields]
        if i > 0:
            left = [back(low_moved[f], low_next[f]) for f in fields]
            new = hll(left, [t[f] - half[f] for f in fields], normal)
            new_moved = [forward(None, new[f]) for f in fields]
            if i > 1:
                emit(i - 2, [forward(flux_moved[f], new_moved[f]) - flux[f] for f in fields])
            flux, flux_moved = new, new_moved
        low_moved = low_next


def groups_of(start, stop):
    return [(at, min(ROWS, stop - at)) for at in range(start, stop, ROWS)]


def y_columns(start, count, skip, blocks, lo_ref, hi_ref, load, add):
    sub = iota((ROWS, LANES), 0)

    def y_back(before, here):
        if before is None:
            return pltpu.roll(here, 1, 0)
        return jnp.where(sub < 1, before, here)

    def y_forward(here, after):
        if here is None:
            return pltpu.roll(after, ROWS - 1, 0)
        return jnp.where(sub >= ROWS - 1, after, here)

    ends = []
    for k in range(count):
        c = start + k
        at = slice((c - skip) // 4 * ROWS, ((c - skip) // 4 + 1) * ROWS)
        if k % 4 == 0:
            low = to_primitive([lo_ref[f, at, :] for f in range(NF)])
            high = to_primitive([hi_ref[f, at, :] for f in range(NF)])
        turn_low, turn_high = (6 - 2 * (k % 4)) % ROWS, (ROWS - 2 * (k % 4)) % ROWS
        below = [pltpu.roll(t, turn_low, 0) if turn_low else t for t in low]
        above = [pltpu.roll(t, turn_high, 0) if turn_high else t for t in high]
        tiles = [load(c, b) for b in range(blocks)]

        def emit(b, change):
            for f in range(NF):
                add(f, c, b, change[f])

        sweep_line(
            [below] + tiles + [above], 1, y_back, y_forward, emit, lambda *end: ends.append(end)
        )
    packed = []
    for which in range(2):
        state = []
        for f in range(NF):
            tile = ends[0][which][f]
            for k in range(1, count):
                tile = jnp.where(sub == k, pltpu.roll(ends[k][which][f], k, 0), tile)
            state.append(tile)
        packed.append(state)
    top = hll(packed[0], packed[1], 1)
    for k in range(count):
        c = start + k
        flux, flux_moved = ends[k][2], ends[k][3]
        for f in range(NF):
            moved = pltpu.roll(top[f], ROWS - 1 - k, 0) if k < ROWS - 1 else top[f]
            change = y_forward(flux_moved[f], moved) - flux[f]
            add(f, c, blocks - 1, change)


def plane_kernel(
    members, msg_ref, lo_ref, hi_ref, fine_ref, after_ref, wz_hbm,
    out_ref, near_ref, wn_ref, sem_ref,
):
    near_copies = [
        pltpu.make_async_copy(
            wz_hbm.at[:, start : start + NEAR],
            near_ref.at[:, i * NEAR : (i + 1) * NEAR],
            sem_ref.at[i],
        )
        for i, start in enumerate((0, PS - NEAR))
    ]
    for copy in near_copies:
        copy.start()
    me = lax.axis_index("dev")
    chunks = fine_ref.shape[2] // LANES
    blocks = fine_ref.shape[1] // ROWS
    lane = iota((ROWS, LANES), 1)
    width = 2 * PS
    place = jnp.full((ROWS, LANES), me, I32)

    def x_back(before, here):
        if before is None:
            return pltpu.roll(here, PS, 1)
        return jnp.where(lane < PS, before, here)

    def x_forward(here, after):
        if here is None:
            return pltpu.roll(after, LANES - PS, 1)
        return jnp.where(lane >= LANES - PS, after, here)

    def x_block(block, carry):
        rows = pl.ds(pl.multiple_of(block * ROWS, ROWS), ROWS)
        left = jnp.maximum(me - 1, 0)
        right = jnp.minimum(me + 1, members - 1)
        shift_low = lax.rem(2 * LANES - width - width * block, LANES)
        shift_high = lax.rem(LANES - width * block, LANES)
        low = to_primitive(
            [pltpu.roll(msg_ref[left, f * ROWS : (f + 1) * ROWS, :], shift_low, 1) for f in range(NF)]
        )
        high = to_primitive(
            [pltpu.roll(msg_ref[right, f * ROWS : (f + 1) * ROWS, :], shift_high, 1) for f in range(NF)]
        )
        tiles = []
        for c in range(chunks):
            prim = to_primitive(
                [fine_ref[f, rows, c * LANES : (c + 1) * LANES] for f in range(NF)]
            )
            for f in range(NF):
                wn_ref[f, c, rows, :] = prim[f]
            tiles.append(prim)
        for f in range(NF):
            w = tiles[0][f]
            same = jnp.where(
                lane < LANES - PS, pltpu.roll(w, LANES - width, 1), pltpu.roll(w, LANES - PS, 1)
            )
            low[f] = jnp.where(place == 0, same, low[f])
            w = tiles[-1][f]
            same = jnp.where(lane < PS, pltpu.roll(w, PS, 1), pltpu.roll(w, width, 1))
            high[f] = jnp.where(place == members - 1, same, high[f])

        def emit(c, change):
            at = slice(c * LANES, (c + 1) * LANES)
            for f in range(NF):
                out_ref[f, c, rows, :] = fine_ref[f, rows, at] - DT_DX * change[f]

        sweep_line([low] + tiles + [high], 0, x_back, x_forward, emit)
        return carry

    lax.fori_loop(0, blocks, x_block, 0)

    def load(c, b):
        return [wn_ref[f, c, b * ROWS : (b + 1) * ROWS, :] for f in range(NF)]

    def add(f, c, b, change):
        at = slice(b * ROWS, (b + 1) * ROWS)
        out_ref[f, c, at, :] = out_ref[f, c, at, :] - DT_DX * change

    for start, count in groups_of(0, Y_EARLY):
        y_columns(start, count, 0, blocks, lo_ref, hi_ref, load, add)
    for copy in near_copies:
        copy.wait()


def face_kernel(
    slot_count, got_ref, code_ref, near_ref, after_ref, term_hbm, edge_hbm,
    edge_ref, he_ref, rt_ref, lf_ref, g_ref, v_ref, term_ref, sem_ref,
):
    lane = iota((ROWS, LANES), 1)
    sub = iota((ROWS, LANES), 0)
    rows_all = NF * QUANT * CF
    y_cells = near_ref.shape[2]
    blocks = y_cells // ROWS
    patch_y = y_cells // PS
    number = iota((CF * slot_count, LANES), 0)
    for i in range(code_ref.shape[0]):
        hot = jnp.where(number == code_ref[i, 0:1, :], 1.0, 0.0)
        he_ref[:, i * LANES : (i + 1) * LANES] = hot.astype(BF16)
    rt_ref[...] = got_ref[...].T
    for cx in range(CF):
        lf_ref[:, cx * slot_count : (cx + 1) * slot_count] = rt_ref[
            pl.ds(cx, rows_all, stride=CF), :
        ]
    parts = jnp.concatenate(split3(lf_ref[...]), axis=0)
    product = jnp.dot(parts, he_ref[...], preferred_element_type=F32)
    g_ref[...] = (
        product[0:rows_all] + product[rows_all : 2 * rows_all] + product[2 * rows_all :]
    )

    def pick(options, index):
        value = jnp.full((ROWS, LANES), options[0], F32)
        for i in range(1, RATIO):
            value = jnp.where(index == i, options[i], value)
        return value

    off_y = pick(OFFSETS, sub % RATIO)
    off_x = pick(OFFSETS, (lane // PS) % RATIO)
    for block in range(blocks):
        ky, half = block // (blocks // patch_y), block % (blocks // patch_y)
        rows = slice(block * ROWS, (block + 1) * ROWS)
        for s in range(SIDES):
            at = (s * patch_y + ky) * LANES
            ghosts = [[], []]
            for f in range(NF):
                terms = []
                for q in range(QUANT):
                    r = (f * QUANT + q) * CF + 2 * half
                    terms.append(
                        jnp.where(
                            sub < RATIO,
                            jnp.broadcast_to(g_ref[r : r + 1, at : at + LANES], (ROWS, LANES)),
                            jnp.broadcast_to(g_ref[r + 1 : r + 2, at : at + LANES], (ROWS, LANES)),
                        )
                    )
                for i in range(2):
                    off_z = OFFSETS[i + (RATIO - 2 if s == 0 else 0)]
                    ghosts[i].append(
                        ((terms[0] + terms[1] * off_z) + terms[2] * off_y) + terms[3] * off_x
                    )

            inner = [
                [near_ref[f, NEAR * s + i, rows, :] for f in range(NF)] for i in range(NEAR)
            ]
            line = ghosts + inner if s == 0 else inner + ghosts
            diff = [[line[i + 1][f] - line[i][f] for f in range(NF)] for i in range(3)]
            half_slope = [
                [0.5 * minmod(diff[i][f], diff[i + 1][f]) for f in range(NF)] for i in range(2)
            ]
            low = [line[1][f] + half_slope[0][f] for f in range(NF)]
            up = [line[2][f] - half_slope[1][f] for f in range(NF)]
            flux = hll(low, up, 2)
            if s == 0:
                state = [line[2][f] + half_slope[1][f] for f in range(NF)]
            else:
                state = [line[1][f] - half_slope[0][f] for f in range(NF)]
            for f in range(NF):
                edge_ref[f, 2 * s, rows, :] = flux[f]
                edge_ref[f, 2 * s + 1, rows, :] = state[f]

    edge_copy = pltpu.make_async_copy(edge_ref, edge_hbm, sem_ref.at[1])
    edge_copy.start()
    v_ref[NF * CF :, :] = jnp.zeros((TERM_ROWS - NF * CF, v_ref.shape[1]), F32)
    for s in range(SIDES):
        for f in range(NF):
            total = None
            for i in range(RATIO):
                got = edge_ref[f, 2 * s, pl.ds(i, y_cells // RATIO, stride=RATIO), :]
                total = got if total is None else total + got
            total = total * (1.0 / RATIO)
            for ky in range(patch_y):
                at = (s * patch_y + ky) * LANES
                v_ref[f * CF : (f + 1) * CF, at : at + LANES] = total[ky * CF : (ky + 1) * CF]
    parts = jnp.concatenate(split3(v_ref[...]), axis=0)
    product = lax.dot_general(
        parts, he_ref[...], (((1,), (1,)), ((), ())), preferred_element_type=F32
    )
    summed = (
        product[0:TERM_ROWS] + product[TERM_ROWS : 2 * TERM_ROWS] + product[2 * TERM_ROWS :]
    )
    turned = summed.T
    for cx in range(CF):
        term_ref[:, cx * TERM_ROWS : (cx + 1) * TERM_ROWS] = turned[
            cx * slot_count : (cx + 1) * slot_count, :
        ]
    copy = pltpu.make_async_copy(term_ref, term_hbm, sem_ref.at[0])
    copy.start()
    edge_copy.wait()
    copy.wait()


def final_kernel(
    fine_hbm, plane_ref, edge_hbm, lo_hbm, hi_hbm, wz_hbm, out_hbm,
    fine_ref, lo_ref, hi_ref, edge_ref, wz_ref, zc_ref, extra_ref, out_ref, wz_sem, out_sem,
):
    lane = iota((ROWS, LANES), 1)
    chunks = plane_ref.shape[1]
    blocks = plane_ref.shape[2] // ROWS

    def wz_copy(block):
        rows = pl.ds(pl.multiple_of(block * ROWS, ROWS), ROWS)
        return pltpu.make_async_copy(
            wz_hbm.at[:, :, rows, :], wz_ref.at[:, :, rows, :], wz_sem.at[block]
        )

    def out_copy(block):
        rows = pl.ds(pl.multiple_of(block * ROWS, ROWS), ROWS)
        return pltpu.make_async_copy(
            out_ref.at[:, rows, :], out_hbm.at[:, rows, :], out_sem.at[block]
        )

    first = Y_EARLY
    edge_copy = pltpu.make_async_copy(edge_hbm, edge_ref, wz_sem.at[blocks])
    late_copies = [
        pltpu.make_async_copy(
            fine_hbm.at[:, :, first * LANES : chunks * LANES], fine_ref, wz_sem.at[blocks + 1]
        ),
        pltpu.make_async_copy(lo_hbm, lo_ref, wz_sem.at[blocks + 2]),
        pltpu.make_async_copy(hi_hbm, hi_ref, wz_sem.at[blocks + 3]),
    ]
    for copy in late_copies:
        copy.start()
    edge_copy.start()
    for block in range(blocks):
        wz_copy(block).start()

    def load(c, b):
        at = slice(b * ROWS, (b + 1) * ROWS)
        lanes = slice((c - first) * LANES, (c - first + 1) * LANES)
        return to_primitive([fine_ref[f, at, lanes] for f in range(NF)])

    def add(f, c, b, change):
        at = slice(b * ROWS, (b + 1) * ROWS)
        extra_ref[f, c - first, at, :] = plane_ref[f, c, at, :] - DT_DX * change

    for copy in late_copies:
        copy.wait()
    for start, count in groups_of(first, chunks):
        y_columns(start, count, 0, blocks, lo_ref, hi_ref, load, add)

    edge_copy.wait()

    def step(block, carry):
        rows = pl.ds(pl.multiple_of(block * ROWS, ROWS), ROWS)
        wz_copy(block).wait()

        def load(z):
            return [wz_ref[f, z, rows, :] for f in range(NF)]

        def edge(i):
            return [edge_ref[f, i, rows, :] for f in range(NF)]

        w_here = load(1)
        w_before = load(0)
        diff = [w_here[f] - w_before[f] for f in range(NF)]
        flux, low = edge(0), edge(1)
        for z in range(1, PS):
            if z < PS - 1:
                w_next = load(z + 1)
                diff_next = [w_next[f] - w_here[f] for f in range(NF)]
                half = [0.5 * minmod(diff[f], diff_next[f]) for f in range(NF)]
                up = [w_here[f] - half[f] for f in range(NF)]
            else:
                up = edge(3)
            new = hll(low, up, 2)
            for f in range(NF):
                zc_ref[f, z - 1] = new[f] - flux[f]
            flux = new
            if z < PS - 1:
                low = [w_here[f] + half[f] for f in range(NF)]
                w_here, diff = w_next, diff_next
        new = edge(2)
        for f in range(NF):
            zc_ref[f, PS - 1] = new[f] - flux[f]
        for f in range(NF):
            tiles = [zc_ref[f, z] for z in range(PS)]
            tiles = swap_groups(tiles, lane)
            for c in range(chunks):
                at = slice(c * LANES, (c + 1) * LANES)
                if c < first:
                    partial = plane_ref[f, c, rows, :]
                else:
                    partial = extra_ref[f, c - first, rows, :]
                out_ref[f, rows, at] = partial - DT_DX * tiles[c]
        out_copy(block).start()
        return carry

    lax.fori_loop(0, blocks, step, 0)

    for block in range(blocks):
        out_copy(block).wait()


def register_kernel(got_ref, hot_ref, out_ref, z_ref):
    boxes = out_ref.shape[2]
    turned = got_ref[...].T
    parts = jnp.concatenate(split3(turned), axis=0)
    product = jnp.dot(parts, hot_ref[...], preferred_element_type=F32)
    z_ref[...] = product[0:LANES] + product[LANES : 2 * LANES] + product[2 * LANES :]
    for f in range(NF):
        for cx in range(CF):
            at = cx * TERM_ROWS + f * CF
            for s in range(SIDES):
                out_ref[f, pl.ds(s * CF * CF + cx, CF, stride=CF), :] = z_ref[
                    at : at + CF, s * boxes : (s + 1) * boxes
                ]


VM = pl.BlockSpec(memory_space=pltpu.VMEM)
HB = pl.BlockSpec(memory_space=pltpu.HBM)
AN = pl.BlockSpec(memory_space=pl.ANY)


def call(body, ins, outs, out_specs, scratch=(), cost=0, limit=8 << 10):
    kernel = pl.pallas_call(
        body,
        in_specs=list(ins),
        out_specs=list(out_specs),
        out_shape=[
            pltpu.HBM(o.shape, o.dtype) if spec is HB else o for o, spec in zip(outs, out_specs)
        ],
        scratch_shapes=list(scratch),
        compiler_params=pltpu.CompilerParams(vmem_limit_bytes=limit << 10),
        cost_estimate=pl.CostEstimate(flops=cost, bytes_accessed=cost, transcendentals=0),
    )

    def run(*args):
        return kernel(
            *[
                pltpu.with_memory_space_constraint(a, pltpu.HBM) if spec is HB else a
                for a, spec in zip(args, ins)
            ]
        )

    return run


def shaped(*shape, dtype=F32):
    return jax.ShapeDtypeStruct(shape, dtype)


def local(members, groups, fine_state, coarse_boxes, piece_owner, piece_box):
    y_cells = fine_state.shape[1]
    x_cells = fine_state.shape[2] // PS
    boxes = coarse_boxes.shape[0]
    pieces = piece_box.shape[0]
    capacity = max(4, 2 * pieces // members)
    slots = members * capacity
    chunks = x_cells * PS // LANES
    blocks = y_cells // ROWS
    patch_y = y_cells // PS
    assert chunks == PS and boxes == LANES and slots <= LANES and PS == QS
    assert y_cells == 4 * ROWS and pieces == SIDES * patch_y * (x_cells // PS)
    edge_rows = 2 * chunks
    rows_all = NF * QUANT * CF
    wide = SIDES * patch_y * LANES
    count = pltpu.SMEM((members,), I32)
    piece_list = pltpu.SMEM((pieces,), I32)
    dma = pltpu.SemaphoreType.DMA
    fine_shape = fine_state.shape
    vmem = lambda *shape: pltpu.VMEM(shape, F32)
    owners = piece_owner.reshape(pieces)

    msg_shape = (members, (NF + 1) * ROWS, LANES)
    edge_shape = (NF, edge_rows, LANES)
    msg, low_edge, high_edge, code = call(
        functools.partial(prep_kernel, members, capacity, boxes),
        (HB, HB, HB),
        [
            shaped(*msg_shape), shaped(*edge_shape), shaped(*edge_shape),
            shaped(SIDES * patch_y, ROWS, LANES, dtype=I32),
        ],
        (HB, HB, HB, VM),
        [
            piece_list, piece_list, count,
            vmem(NF, ROWS, fine_shape[2]), vmem(NF, ROWS, fine_shape[2]),
            vmem(NF, y_cells, LANES), vmem(NF, y_cells, LANES),
            vmem(*msg_shape), vmem(*edge_shape), vmem(*edge_shape),
            dma((6,)), dma((3,)),
        ],
        cost=1 << 18,
    )(owners, piece_box, fine_state)
    got = lax.all_to_all(msg, "dev", split_axis=0, concat_axis=0, tiled=True)
    up = [(g, (g + 1) % groups) for g in range(groups)]
    down = [(b, a) for a, b in up]
    y_low = lax.ppermute(high_edge, "group", up)
    y_high = lax.ppermute(low_edge, "group", down)

    turned_shape = (NF, PS, y_cells, LANES)
    build = call(
        build_kernel,
        (VM, HB),
        [
            shaped(*turned_shape),
            shaped(TABLE_ROWS, SIDES * boxes),
        ],
        (HB, VM),
        [
            vmem(NF, chunks, ROWS, LANES),
            vmem(*turned_shape),
            vmem(NF, boxes, CB * CB * CB),
            vmem(NF, CB * CB * CB, boxes),
            dma((NF,)),
            dma((1,)),
        ],
        cost=1 << 23,
    )
    wz, table = build(fine_state, coarse_boxes.transpose(1, 0, 2))
    payload, hot_box = call(
        serve_kernel,
        (VM, VM),
        [shaped(slots, TABLE_PAD), shaped(slots, SIDES * boxes, dtype=BF16)],
        (HB, VM),
        [vmem(slots, TABLE_PAD), dma((1,))],
        cost=1 << 18,
    )(got, table)
    back = lax.all_to_all(payload, "dev", split_axis=0, concat_axis=0, tiled=True)

    plane, near = call(
        functools.partial(plane_kernel, members),
        (VM, VM, VM, VM, VM, HB),
        [
            shaped(NF, chunks, y_cells, LANES),
            shaped(NF, 2 * NEAR, y_cells, LANES),
        ],
        (VM, VM),
        [
            vmem(NF, chunks, y_cells, LANES),
            dma((2,)),
        ],
        cost=1 << 24,
    )(got, y_low, y_high, fine_state, hot_box, wz)

    terms, edge = call(
        functools.partial(face_kernel, slots),
        (VM, VM, VM, VM),
        [shaped(slots, LANES), shaped(NF, 4, y_cells, LANES)],
        (HB, HB),
        [
            vmem(NF, 4, y_cells, LANES),
            pltpu.VMEM((CF * slots, wide), BF16),
            vmem(TABLE_PAD, slots),
            vmem(rows_all, CF * slots),
            vmem(rows_all, wide),
            vmem(TERM_ROWS, wide),
            vmem(slots, LANES),
            dma((2,)),
        ],
        cost=1 << 20,
    )(back, code, near, plane)
    incoming = lax.all_to_all(terms, "dev", split_axis=0, concat_axis=0, tiled=True)

    late = chunks - Y_EARLY
    (fine_next,) = call(
        final_kernel,
        (HB, VM, HB, AN, AN, HB),
        [shaped(*fine_shape)],
        (HB,),
        [
            vmem(NF, y_cells, late * LANES),
            vmem(*edge_shape),
            vmem(*edge_shape),
            vmem(NF, 4, y_cells, LANES),
            vmem(*turned_shape),
            vmem(NF, PS, ROWS, LANES),
            vmem(NF, late, y_cells, LANES),
            vmem(*fine_shape),
            dma((blocks + 4,)),
            dma((blocks,)),
        ],
        cost=1 << 24,
    )(fine_state, plane, edge, y_low, y_high, wz)
    (flux_register,) = call(
        register_kernel,
        (VM, VM),
        [shaped(NF, SIDES * CF * CF, boxes)],
        (VM,),
        [vmem(LANES, SIDES * boxes)],
        cost=1 << 18,
    )(incoming, hot_box)
    return (fine_next, flux_register)


def solution(mesh):
    in_specs = (
        P(None, "group", "dev"),
        P(("group", "dev"), None, None),
        P(("group", "dev"), None),
        P(("group", "dev")),
    )
    out_specs = (P(None, "group", "dev"), P(None, None, ("group", "dev")))
    body = functools.partial(local, mesh.shape["dev"], mesh.shape["group"])
    return jax.shard_map(body, mesh=mesh, in_specs=in_specs, out_specs=out_specs, check_vma=False)
```
